128 devices in a mesh: row: 16 (over x, z), col: 8 (over y, core).
Axes of the slice: x: 4, y: 4, z: 4, core: 2. Of those that a mesh axis runs over, the one named last changes fastest.
Arguments:
- innovations: float32 [64, 65536], P(None, ('row', 'col')), may hold values from -300 to 300
- obs_factors: float32 [64, 65536], P(None, ('row', 'col')), may hold values from -6 to 6
- component: int32 [65536], P(('row', 'col')), may hold values 0 or 1
- obs_error: float32 [65536], P(('row', 'col')), may hold values from 0.5 to 2
- coupling: float32 [2, 2], replicated, may hold values from 0.5 to 2
- tile_slots: int32 [16, 8, 8, 3], P('row', 'col'), may hold values from 0 to 15, as said below
Outputs:
- increment: float32 [64, 65536], P(None, ('row', 'col'))
- residual: float32 [64, 65536], P(None, ('row', 'col'))
The draws below stay inside these ranges and needn't reach their ends.
Inputs may be any that keep to these rules, and one draw needn't show every extreme that they name: `tile_slots`: each device's slots name distinct (local block row, local block column) pairs; on some device all 8 slots are live; the live flag is 0 or 1; local block rows are below 8 and local block columns below 16.
All inputs are finite; a program needn't handle non-finite values. No bound on the sum of `component` on one device may be relied on, other than what follows from the above.
Results may differ from the reference program's by a relative error of at most 0.0003.
Values sent between devices are 32-bit elements; how exact they have to be, the bound alone decides.
No kernel may reach another device: no remote copies, remote signals or barrier semaphores. Data moves between devices by JAX's collectives and lax.ppermute only.
A program may use at most 64 MiB of HBM per device.

```python
import math
import jax
import jax.numpy as jnp
from jax import lax

TILE = 512
DF = 64
NRHS = 64
ITERS = 3
SLOTS = 8
BLK_DEV = 1
ROW_DEVS = 16
COL_DEVS = 8
NR_LOC = 8
NC_LOC = 16
NOBS = 65536


def factor_field(key):
    factor_key = jax.random.fold_in(key, 7)
    field = jnp.clip(jax.random.normal(factor_key, (DF, NOBS), jnp.float32), -6.0, 6.0)
    return field


def draw_obs_factors(key, part):
    return factor_field(key)


def draw_innovations(key, part):
    first_key = jax.random.fold_in(jax.random.fold_in(key, 3), 0)
    third_key = jax.random.fold_in(jax.random.fold_in(key, 3), 2)
    position = jnp.arange(NOBS, dtype=jnp.float32) / NOBS
    rising = jnp.exp(math.log(3.0) * position)
    loadings = jax.random.normal(third_key, (NRHS, DF), jnp.float32)
    coherent = jnp.dot(loadings, factor_field(key), precision=lax.Precision.HIGHEST) / math.sqrt(DF)
    noise_part = jnp.clip(jax.random.normal(first_key, (NRHS, NOBS), jnp.float32), -6.0, 6.0)
    coherent = jnp.clip(coherent, -6.0, 6.0)
    mixed = 0.5 * noise_part + 0.85 * coherent
    return mixed * rising[None, :]


def draw_tile_slots(key, part):
    first_key, second_key, third_key = jax.random.split(jax.random.fold_in(key, 11), 3)
    devices = ROW_DEVS * COL_DEVS
    cells = NR_LOC * NC_LOC
    scores = jax.random.randint(first_key, (devices, cells), 0, 65536) * cells + jnp.arange(cells, dtype=jnp.int32)[None, :]
    chosen = jnp.argsort(scores, axis=1)[:, :SLOTS].astype(jnp.int32)
    spread = SLOTS - SLOTS // 6
    extra = jax.random.randint(second_key, (devices,), 0, spread + 1)
    counts = SLOTS // 6 + extra * extra // max(spread, 1)
    picked = jax.random.randint(third_key, (), 0, devices)
    counts = jnp.where(jnp.arange(devices, dtype=jnp.int32) == picked, SLOTS, counts)
    live_flags = (jnp.arange(SLOTS, dtype=jnp.int32)[None, :] < counts[:, None]).astype(jnp.int32)
    stacked = jnp.stack([chosen // NC_LOC, chosen % NC_LOC, live_flags], axis=-1)
    return stacked.reshape(ROW_DEVS, COL_DEVS, SLOTS, 3).astype(jnp.int32)


def with_ends(values, own_key, least, high):
    spot = [jax.random.randint(jax.random.fold_in(own_key, axis), (), 0, length) for axis, length in enumerate(values.shape)]
    widest = values.shape.index(max(values.shape))
    beside = spot[:widest] + [(spot[widest] + 1) % values.shape[widest]] + spot[widest + 1:]
    return values.at[tuple(spot)].set(least).at[tuple(beside)].set(high)


def levels(rng, dims, shards, smallest, largest):
    factor_of = 1.0
    for dim, shards_of in shards:
        heights = jax.random.uniform(jax.random.fold_in(jax.random.fold_in(rng, 6), dim), (shards_of,), jnp.float32, smallest / len(shards), largest / len(shards))
        factor_of = factor_of * jnp.repeat(jnp.exp(heights), dims[dim] // shards_of).reshape((-1,) + (1,) * (len(dims) - 1 - dim))
    return factor_of


def setup_inputs(seed: int = 0) -> dict:
    arg_keys = jax.random.split(jax.random.key(seed), 7)
    return {
        "innovations": draw_innovations(jax.random.fold_in(arg_keys[6], 71), 0),
        "obs_factors": draw_obs_factors(jax.random.fold_in(arg_keys[6], 71), 0),
        "component": with_ends((jax.random.randint(arg_keys[2], (NOBS,), 0, 4) < 1).astype(jnp.int32), jax.random.fold_in(arg_keys[2], 1), 0, 1),
        "obs_error": jnp.clip(jnp.exp(math.log(2.0) - 1.3862944 * jax.random.uniform(arg_keys[3], (NOBS,), jnp.float32) ** levels(arg_keys[3], (NOBS,), ((0, 128),), -0.2, 0.2)), 0.5, 2.0),
        "coupling": jnp.clip(jnp.exp(jax.random.uniform(arg_keys[4], (2, 2), jnp.float32, math.log(0.5), math.log(2.0))), 0.5, 2.0),
        "tile_slots": draw_tile_slots(jax.random.fold_in(arg_keys[6], 71), 0),
    }


length_sq = 12.0


def tile_matrix(left_factors, right_factors, left_labels, right_labels, coupling):
    left_norms = jnp.sum(left_factors * left_factors, axis=0)
    right_norms = jnp.sum(right_factors * right_factors, axis=0)
    products = lax.dot_general(left_factors, right_factors, (((0,), (0,)), ((), ())), precision=lax.Precision.HIGHEST, preferred_element_type=jnp.float32)
    pair_coupling = (1.0 - left_labels)[:, None] * ((1.0 - right_labels)[None, :] * coupling[0, 0] + right_labels[None, :] * coupling[0, 1]) + left_labels[:, None] * ((1.0 - right_labels)[None, :] * coupling[1, 0] + right_labels[None, :] * coupling[1, 1])
    return pair_coupling * jnp.exp(-(left_norms[:, None] + right_norms[None, :] - 2.0 * products) / length_sq)


def take_segment(array, block):
    start = (block * TILE).astype(jnp.int32)
    return lax.dynamic_slice_in_dim(array, start, TILE, array.ndim - 1)


def add_segment(vector, block, values):
    start = (block * TILE).astype(jnp.int32)
    last_axis = vector.ndim - 1
    before = lax.dynamic_slice_in_dim(vector, start, TILE, last_axis)
    return lax.dynamic_update_slice_in_dim(vector, before + values, start, last_axis)


def reference(innovations, obs_factors, component, obs_error, coupling, tile_slots):
    labels_float = component.astype(jnp.float32)
    row_devices = jnp.arange(ROW_DEVS, dtype=jnp.int32)[:, None, None]
    column_devices = jnp.arange(COL_DEVS, dtype=jnp.int32)[None, :, None]
    row_block = tile_slots[..., 0]
    column_block = tile_slots[..., 1]
    global_rows = ((row_devices * COL_DEVS + row_block // BLK_DEV) * BLK_DEV + row_block % BLK_DEV).reshape(-1).astype(jnp.int32)
    global_columns = (((column_block // BLK_DEV) * COL_DEVS + column_devices) * BLK_DEV + column_block % BLK_DEV).reshape(-1).astype(jnp.int32)
    live_list = tile_slots[..., 2].reshape(-1).astype(jnp.int32)

    def listed_tile(row_index, column_index):
        return tile_matrix(take_segment(obs_factors, row_index), take_segment(obs_factors, column_index), take_segment(labels_float, row_index), take_segment(labels_float, column_index), coupling)

    def weigh(totals, item):
        row_index, column_index, flag = item

        def work(totals):
            block_matrix = listed_tile(row_index, column_index)
            totals = add_segment(totals, row_index, jnp.sum(block_matrix, axis=1))
            return add_segment(totals, column_index, jnp.sum(block_matrix, axis=0))

        return lax.cond(flag > 0, work, lambda totals: totals, totals), None

    row_weights, unused = lax.scan(weigh, jnp.zeros((NOBS,), jnp.float32), (global_rows, global_columns, live_list))
    diagonal = obs_error + row_weights

    def operate(vector):
        def visit(totals, item):
            row_index, column_index, flag = item

            def work(totals):
                block_matrix = listed_tile(row_index, column_index)
                left_values = take_segment(vector, row_index)
                right_values = take_segment(vector, column_index)
                totals = add_segment(totals, row_index, lax.dot_general(right_values, block_matrix, (((1,), (1,)), ((), ())), precision=lax.Precision.HIGHEST, preferred_element_type=jnp.float32))
                return add_segment(totals, column_index, jnp.dot(left_values, block_matrix, precision=lax.Precision.HIGHEST, preferred_element_type=jnp.float32))

            return lax.cond(flag > 0, work, lambda totals: totals, totals), None

        image, unused = lax.scan(visit, jnp.zeros((NRHS, NOBS), jnp.float32), (global_rows, global_columns, live_list))
        return diagonal[None, :] * vector + image

    increment = jnp.zeros_like(innovations)
    residual = innovations
    direction = innovations
    norm_now = jnp.sum(residual * residual, axis=1)
    for repeat in range(ITERS):
        image = operate(direction)
        alpha = norm_now / jnp.sum(direction * image, axis=1)
        increment = increment + alpha[:, None] * direction
        residual = residual - alpha[:, None] * image
        norm_next = jnp.sum(residual * residual, axis=1)
        direction = residual + (norm_next / norm_now)[:, None] * direction
        norm_now = norm_next
    return increment, residual
```

```python
import functools
import math

import jax
import jax.numpy as jnp
from jax import lax
from jax.experimental import pallas as pl
from jax.experimental.pallas import tpu as pltpu
from jax.sharding import Mesh
from jax.sharding import PartitionSpec as P

TILE = 512
X, Z, Y, C = "row_0", "row_1", "col_0", "col_1"
ALL = (X, Z, Y, C)
ROW, COL = (X, Z), (Y, C)
BODY = 256
ROWS = BODY + 8
KEPT = 32
LISTED = 136
SLOTS_OUT = 144
KAPPA = math.log2(math.e) / 12.0
F32, BF16 = jnp.float32, jnp.bfloat16


def along_row(stage, step):
    pairs = []
    for x in range(4):
        for z in range(4):
            for y in range(4):
                for c in range(2):
                    if (c == 0) == (stage == 1):
                        to = ((x + step) % 4, z)
                    else:
                        to = (x, (z + step) % 4)
                    pairs.append((((x * 4 + z) * 4 + y) * 2 + c, ((to[0] * 4 + to[1]) * 4 + y) * 2 + c))
    return pairs


def hop(a, stage, step):
    return lax.ppermute(a, ALL, along_row(stage, step))


def gather_row(block):
    far = hop(block, 1, 2)
    ahead = hop(block, 1, -1)
    behind = hop(block, 1, 1)
    line = jnp.stack([block, ahead, far, behind])
    right = hop(line, 2, -1)
    left = hop(line, 2, 1)
    far_left = hop(left[:2], 2, 1)
    far_right = hop(right[2:], 2, -1)
    return line, right, far_left, far_right, left


def shift_y(a, step):
    return lax.ppermute(a, Y, [(i, (i + step) % 4) for i in range(4)])


def reduce_col(keep, other):
    got = lax.ppermute(other, C, [(0, 1), (1, 0)])
    parts = [keep[j] + got[j] for j in range(4)]
    return parts[0], shift_y(parts[2], 2), shift_y(parts[1], 1), shift_y(parts[3], -1)


def halves(v):
    h = v.astype(BF16).astype(F32)
    m = (v - h).astype(BF16).astype(F32)
    return h, m, v - h - m


def rows_of(values, count, width):
    at = lax.broadcasted_iota(jnp.int32, (count, width), 0)
    out = jnp.zeros((count, width), F32)
    for k, value in enumerate(values):
        out = jnp.where(at == k, value, out)
    return out


def make_tile(fin, lin, fout, lout, turned, lc_ref, e_ref, pair_ref):
    h, m, l = halves(fin)
    norms = halves(-KAPPA * jnp.sum(fin * fin, axis=0, keepdims=True))
    aug = rows_of([*norms, 1.0, 1.0, 1.0, *[1.0 - lin, lin] * 3], 16, TILE)
    hm = jnp.concatenate([h, m], axis=0).T.astype(BF16)
    hl = jnp.concatenate([h, l], axis=0).T.astype(BF16)
    au = jnp.concatenate([aug, jnp.zeros((112, TILE), F32)], axis=0).T.astype(BF16)
    left = jnp.concatenate([hm, hm, hl, au], axis=1)
    g, n, k = halves(fout * (2.0 * KAPPA))
    norms = halves(-KAPPA * jnp.sum(fout * fout, axis=0, keepdims=True))
    levels = []
    for i in range(2):
        first = jnp.where(turned, lc_ref[2 * i], lc_ref[i])
        second = jnp.where(turned, lc_ref[2 * i + 1], lc_ref[2 + i])
        levels.append(halves(jnp.where(lout > 0.5, second, first)))
    logs = [levels[i][j] for j in range(3) for i in range(2)]
    aug = rows_of([1.0, 1.0, 1.0, *norms, *logs], 16, TILE)
    right = jnp.concatenate([g, g, n, n, k, g, aug, jnp.zeros((112, TILE), F32)], axis=0).astype(BF16)
    e_ref[...] = jnp.dot(left, right, preferred_element_type=F32)
    total = jnp.zeros((8, TILE), F32)
    for at in range(0, TILE, 64):
        t = jnp.exp2(e_ref[at : at + 64, :])
        hi = t.astype(BF16)
        pair_ref[0, at : at + 64, :] = hi
        pair_ref[1, at : at + 64, :] = (t - hi.astype(F32)).astype(BF16)
        total = total + jnp.sum(t.reshape(8, 8, TILE), axis=0)
    return jnp.sum(total, axis=0, keepdims=True)


def add_product(xs_ref, place, pair_ref, acc_ref, k):
    x = xs_ref[place]
    both = jnp.dot(x, pair_ref[0], preferred_element_type=F32)
    low = jnp.dot(x[:64], pair_ref[1], preferred_element_type=F32)
    out = both[:64] + both[64:] + low
    for g in range(4):
        acc_ref[k, g * 64 : g * 64 + 64, :] += out[:, g * 128 : g * 128 + 128]


def split_into(xs_ref, place, lanes, value):
    hi = value.astype(BF16)
    xs_ref[place, 0:64, lanes] = hi
    xs_ref[place, 64:128, lanes] = (value - hi.astype(F32)).astype(BF16)


def unpack(entry):
    return entry & 7, (entry >> 3) & 15, ((entry >> 7) & 1) == 1, entry >> 8


def first_kernel(
    info_ref, lc_ref, line, right, far_left, far_right, left, outs_ref,
    keep_ref, other_ref, list_ref, store_ref, facts_ref,
    fin_ref, xs_ref, e_ref, pair_ref, acc_ref, sems, fact_sem,
):
    place = 0
    for piece in (line, right, far_left, far_right, left):
        for j in range(piece.shape[0]):
            fin_ref[place, 0:64, :] = piece[j, 0:64, :]
            fin_ref[place, 64:72, :] = piece[j, 128:136, :]
            split_into(xs_ref, place, slice(None), piece[j, 64:128, :])
            place += 1
    facts = pltpu.make_async_copy(fin_ref, facts_ref, fact_sem)
    facts.start()
    acc_ref[...] = jnp.zeros_like(acc_ref)

    def enlist(i, n):
        list_ref[n] = info_ref[0, i]
        return n + info_ref[1, i]

    n = lax.fori_loop(0, LISTED, enlist, jnp.int32(0), unroll=8)
    list_ref[SLOTS_OUT - 1] = n

    def saved(t):
        slot = t & 1
        return pltpu.make_async_copy(pair_ref.at[slot], store_ref.at[jnp.minimum(t, KEPT - 1)], sems.at[slot])

    def visit(t, carry):
        k, place, turned, block = unpack(list_ref[t])
        slot = t & 1

        @pl.when((t >= 2) & (t - 2 < KEPT))
        def _():
            saved(t - 2).wait()

        pair = pair_ref.at[slot]
        sums = make_tile(
            fin_ref[place, 0:64, :], fin_ref[place, 64:65, :], outs_ref[block, 0:64, :], outs_ref[block, 64:65, :],
            turned, lc_ref, e_ref, pair,
        )

        @pl.when(t < KEPT)
        def _():
            saved(t).start()

        add_product(xs_ref, place, pair, acc_ref, k)
        spread = jnp.concatenate([sums[:, g * 128 : g * 128 + 128] for g in range(4)] + [jnp.zeros((4, 128), F32)], axis=0)
        acc_ref[k, BODY:ROWS, :] += spread
        return carry

    lax.fori_loop(0, n, visit, jnp.int32(0))
    for back in (2, 1):

        @pl.when((n >= back) & (n - back < KEPT))
        def _():
            saved(n - back).wait()

    keep_ref[...] = acc_ref[0:4]
    other_ref[...] = acc_ref[4:8]
    facts.wait()


DEPTH = 4


def operate_kernel(
    list_ref, lc_ref, line, right, far_left, far_right, left, store_ref, facts_ref, outs_ref,
    keep_ref, other_ref,
    fin_ref, fout_ref, xs_ref, e_ref, pair_ref, acc_ref, sems, fact_sems,
):
    n = list_ref[SLOTS_OUT - 1]
    kept = jnp.minimum(n, KEPT)

    def loaded(t):
        slot = t & (DEPTH - 1)
        return pltpu.make_async_copy(store_ref.at[jnp.minimum(t, KEPT - 1)], pair_ref.at[slot], sems.at[slot])

    for t in range(DEPTH):

        @pl.when(t < kept)
        def _():
            loaded(t).start()

    place = 0
    sums = jnp.zeros((8, 128), F32)
    for piece in (line, right, far_left, far_right, left):
        for j in range(piece.shape[0]):
            for g in range(4):
                split_into(xs_ref, place, slice(g * 128, g * 128 + 128), piece[j, g * 64 : g * 64 + 64, :])
            sums = sums + piece[j, BODY:ROWS, :]
            place += 1
    acc_ref[...] = jnp.zeros_like(acc_ref)
    for k in range(8):
        acc_ref[k, BODY:ROWS, :] = sums

    def visit(t, carry):
        k, place, _, _ = unpack(list_ref[t])
        loaded(t).wait()
        add_product(xs_ref, place, pair_ref.at[t & (DEPTH - 1)], acc_ref, k)

        @pl.when(t + DEPTH < kept)
        def _():
            loaded(t + DEPTH).start()

        return carry

    lax.fori_loop(0, kept, visit, jnp.int32(0))

    def visit_again(t, carry):
        k, place, turned, block = unpack(list_ref[t])
        first = pltpu.make_async_copy(facts_ref.at[place], fin_ref, fact_sems.at[0])
        second = pltpu.make_async_copy(outs_ref.at[block], fout_ref, fact_sems.at[1])
        first.start()
        second.start()
        first.wait()
        second.wait()
        pair = pair_ref.at[0]
        make_tile(fin_ref[0:64, :], fin_ref[64:65, :], fout_ref[0:64, :], fout_ref[64:65, :], turned, lc_ref, e_ref, pair)
        add_product(xs_ref, place, pair, acc_ref, k)
        return carry

    lax.fori_loop(kept, n, visit_again, jnp.int32(0))
    keep_ref[...] = acc_ref[0:4]
    other_ref[...] = acc_ref[4:8]


def group(g):
    return slice(g * 64, g * 64 + 64)


def lanes(g):
    return slice(g * 128, g * 128 + 128)


def sum_rows(first, second):
    both = jnp.concatenate([first, second], axis=0)
    column = jnp.broadcast_to(jnp.sum(both, axis=1, keepdims=True), (128, 128))
    return column.T[0:8, :]


def columns_of(row):
    turned = jnp.broadcast_to(row, (128, 128)).T
    return turned[0:64], turned[64:128]


def total_of(parts, rows):
    a, b, c, d = parts
    return (a[rows, :] + b[rows, :]) + (c[rows, :] + d[rows, :])


def after_first(a, b, c, d, r_ref, err_ref, w_ref, diag_ref):
    parts = (a, b, c, d)
    diag = err_ref[0:4, :] + total_of(parts, slice(BODY, BODY + 4))
    diag_ref[0:4, :] = diag
    diag_ref[4:8, :] = jnp.zeros((4, 128), F32)
    rr, rw = jnp.zeros((64, 128), F32), jnp.zeros((64, 128), F32)
    for g in range(4):
        r = r_ref[:, lanes(g)]
        w = diag[g : g + 1, :] * r + total_of(parts, group(g))
        w_ref[group(g), :] = w
        rr, rw = rr + r * r, rw + r * w
    w_ref[BODY:ROWS, :] = sum_rows(rr, rw)


def after_second(a, b, c, d, r_ref, w_ref, diag_ref, next_ref, r1_ref, q_ref, past_ref):
    parts = (a, b, c, d)
    rr0, rw0 = columns_of(total_of(parts, slice(BODY, BODY + 1)))
    alpha = rr0 / rw0
    past_ref[0:64, :] = alpha
    past_ref[64:128, :] = rr0
    rr, rw = jnp.zeros((64, 128), F32), jnp.zeros((64, 128), F32)
    for g in range(4):
        w0 = w_ref[group(g), :]
        q = diag_ref[g : g + 1, :] * w0 + total_of(parts, group(g))
        r = r_ref[:, lanes(g)] - alpha * w0
        w = w0 - alpha * q
        q_ref[group(g), :] = q
        r1_ref[group(g), :] = r
        next_ref[group(g), :] = w
        rr, rw = rr + r * r, rw + r * w
    next_ref[BODY:ROWS, :] = sum_rows(rr, rw)


def after_third(
    a, b, c, d, r_ref, w0_ref, diag_ref, w1_ref, r1_ref, q_ref, past_ref,
    sums_ref, r2_ref, w2_ref, s1_ref, p1_ref, x_ref, now_ref,
):
    parts = (a, b, c, d)
    rr1, rw1 = columns_of(total_of(parts, slice(BODY, BODY + 1)))
    alpha0, rr0 = past_ref[0:64, :], past_ref[64:128, :]
    beta = rr1 / rr0
    alpha = rr1 / (rw1 - beta * rr1 / alpha0)
    now_ref[0:64, :] = alpha
    now_ref[64:128, :] = rr1
    rr, rw = jnp.zeros((64, 128), F32), jnp.zeros((64, 128), F32)
    for g in range(4):
        w1, r1, r0 = w1_ref[group(g), :], r1_ref[group(g), :], r_ref[:, lanes(g)]
        q1 = diag_ref[g : g + 1, :] * w1 + total_of(parts, group(g))
        s = w1 + beta * w0_ref[group(g), :]
        z = q1 + beta * q_ref[group(g), :]
        p = r1 + beta * r0
        r = r1 - alpha * s
        w = w1 - alpha * z
        s1_ref[group(g), :] = s
        p1_ref[group(g), :] = p
        x_ref[group(g), :] = alpha0 * r0 + alpha * p
        r2_ref[group(g), :] = r
        w2_ref[group(g), :] = w
        rr, rw = rr + r * r, rw + r * w
    sums_ref[...] = sum_rows(rr, rw)


def finish(sums_ref, r2_ref, w2_ref, s1_ref, p1_ref, x_ref, now_ref, inc_ref, res_ref):
    rr2, rw2 = columns_of(sums_ref[...])
    alpha1, rr1 = now_ref[0:64, :], now_ref[64:128, :]
    beta = rr2 / rr1
    alpha = rr2 / (rw2 - beta * rr2 / alpha1)
    for g in range(4):
        r = r2_ref[group(g), :]
        p = r + beta * p1_ref[group(g), :]
        s = w2_ref[group(g), :] + beta * s1_ref[group(g), :]
        inc_ref[:, lanes(g)] = x_ref[group(g), :] + alpha * p
        res_ref[:, lanes(g)] = r - alpha * s


VMEM = pl.BlockSpec(memory_space=pltpu.VMEM)
SMEM = pl.BlockSpec(memory_space=pltpu.SMEM)
ANY = pl.BlockSpec(memory_space=pl.ANY)


def small_call(body, shapes, args):
    out = [jax.ShapeDtypeStruct(s, F32) for s in shapes]
    return pl.pallas_call(
        body,
        out_shape=out,
        in_specs=[VMEM] * len(args),
        out_specs=[VMEM] * len(shapes),
        cost_estimate=pl.CostEstimate(flops=4_000_000, bytes_accessed=2_000_000, transcendentals=0),
    )(*args)


PART = jax.ShapeDtypeStruct((4, ROWS, 128), F32)


def first_operate(info, log_coupling, pieces, outs):
    return pl.pallas_call(
        first_kernel,
        out_shape=[
            PART,
            PART,
            jax.ShapeDtypeStruct((SLOTS_OUT,), jnp.int32),
            jax.ShapeDtypeStruct((KEPT, 2, TILE, TILE), BF16),
            jax.ShapeDtypeStruct((16, 72, TILE), F32),
        ],
        in_specs=[SMEM, SMEM] + [VMEM] * 6,
        out_specs=[VMEM, VMEM, SMEM, ANY, ANY],
        scratch_shapes=[
            pltpu.VMEM((16, 72, TILE), F32),
            pltpu.VMEM((16, 128, TILE), BF16),
            pltpu.VMEM((TILE, TILE), F32),
            pltpu.VMEM((2, 2, TILE, TILE), BF16),
            pltpu.VMEM((8, ROWS, 128), F32),
            pltpu.SemaphoreType.DMA((2,)),
            pltpu.SemaphoreType.DMA,
        ],
        compiler_params=pltpu.CompilerParams(vmem_limit_bytes=40 << 20),
        cost_estimate=pl.CostEstimate(flops=8_000_000_000, bytes_accessed=20_000_000, transcendentals=2_000_000),
    )(info, log_coupling, *pieces, outs)


def later_operate(listed, log_coupling, pieces, store, facts, outs):
    return pl.pallas_call(
        operate_kernel,
        out_shape=[PART, PART],
        in_specs=[SMEM, SMEM] + [VMEM] * 5 + [ANY] * 3,
        out_specs=[VMEM, VMEM],
        scratch_shapes=[
            pltpu.VMEM((72, TILE), F32),
            pltpu.VMEM((72, TILE), F32),
            pltpu.VMEM((16, 128, TILE), BF16),
            pltpu.VMEM((TILE, TILE), F32),
            pltpu.VMEM((DEPTH, 2, TILE, TILE), BF16),
            pltpu.VMEM((8, ROWS, 128), F32),
            pltpu.SemaphoreType.DMA((DEPTH,)),
            pltpu.SemaphoreType.DMA((2,)),
        ],
        compiler_params=pltpu.CompilerParams(vmem_limit_bytes=40 << 20),
        cost_estimate=pl.CostEstimate(flops=4_000_000_000, bytes_accessed=12_000_000, transcendentals=0),
    )(listed, log_coupling, *pieces, store, facts, outs)


def worklist(slots, seen, place):
    x, z, y, c = place
    mine = 128 + (y * 2 + c) * 16 + x * 4 + z
    turned = jnp.any(seen == mine, axis=1).astype(jnp.int32)
    index = jnp.arange(128, dtype=jnp.int32)
    a = jnp.concatenate([slots[:, 0], index & 7])
    b = jnp.concatenate([slots[:, 1], index >> 3])
    flag = jnp.concatenate([jnp.zeros((8,), jnp.int32), jnp.ones((128,), jnp.int32)])
    k = ((a & 1) ^ c) * 4 + (((a >> 1) - y) & 3)
    dx, dz = ((b >> 2) - x) & 3, ((b & 3) - z) & 3
    s1, s2 = jnp.where(c == 0, dx, dz), jnp.where(c == 0, dz, dx)
    entry = k + 8 * (s2 * 4 + s1) + 128 * flag + 256 * a
    live = jnp.concatenate([slots[:, 2], turned])
    return jnp.pad(jnp.stack([entry, live]), ((0, 0), (0, SLOTS_OUT - LISTED)))


def to_everyone(row, count, axes):
    copies = jnp.broadcast_to(row.reshape(1, 1, 128), (count, 1, 128))
    return lax.all_to_all(copies, axes, split_axis=0, concat_axis=0, tiled=True)


def shards(innovations, obs_factors, component, obs_error, coupling, tile_slots):
    place = tuple(lax.axis_index(axis) for axis in ALL)
    labels = jnp.broadcast_to(component.astype(F32)[None, :], (8, TILE))
    payload = jnp.concatenate([obs_factors, innovations, labels], axis=0)
    pieces = gather_row(payload)
    facts = jnp.concatenate([obs_factors, labels], axis=0)
    copies = jnp.broadcast_to(facts[None], (8, *facts.shape))
    outs = lax.all_to_all(copies, COL, split_axis=0, concat_axis=0, tiled=True)
    slots = tile_slots[0, 0]
    code = slots[:, 2] * 128 + slots[:, 0] * 16 + slots[:, 1]
    seen = to_everyone(jnp.pad(code, (0, 120)), 128, ALL)[:, 0, 0:8]
    info = worklist(slots, seen, place)
    log_coupling = jnp.log2(coupling).reshape(4)
    error_rows = jnp.pad(obs_error.reshape(4, 128), ((0, 4), (0, 0)))

    vec, body, two = (ROWS, 128), (BODY, 128), (128, 128)
    keep, other, listed, store, kept_facts = first_operate(info, log_coupling, pieces, outs)
    parts = reduce_col(keep, other)
    w0, diag = small_call(after_first, [vec, (8, 128)], (*parts, innovations, error_rows))

    keep, other = later_operate(listed, log_coupling, gather_row(w0), store, kept_facts, outs)
    parts = reduce_col(keep, other)
    w1, r1, q0, past = small_call(after_second, [vec, body, body, two], (*parts, innovations, w0, diag))

    keep, other = later_operate(listed, log_coupling, gather_row(w1), store, kept_facts, outs)
    parts = reduce_col(keep, other)
    sums, r2, w2, s1, p1, x2, now = small_call(
        after_third,
        [(8, 128), body, body, body, body, body, two],
        (*parts, innovations, w0, diag, w1, r1, q0, past),
    )
    sums = jnp.sum(to_everyone(sums[0:1], 128, ALL), axis=0)
    increment, residual = small_call(finish, [(64, TILE)] * 2, (sums, r2, w2, s1, p1, x2, now))
    return increment, residual


def solution(mesh):
    finer = Mesh(mesh.devices.reshape(4, 4, 4, 2), ALL)
    in_specs = (P(None, ALL), P(None, ALL), P(ALL), P(ALL), P(), P(ROW, COL, None, None))
    out_specs = (P(None, ALL), P(None, ALL))
    return jax.shard_map(shards, mesh=finer, in_specs=in_specs, out_specs=out_specs, check_vma=False)
```

```python
import functools
import math

import jax
import jax.numpy as jnp
from jax import lax
from jax.experimental import pallas as pl
from jax.experimental.pallas import tpu as pltpu
from jax.sharding import Mesh
from jax.sharding import PartitionSpec as P

TILE = 512
X, Z, Y, C = "row_0", "row_1", "col_0", "col_1"
ALL = (X, Z, Y, C)
ROW, COL = (X, Z), (Y, C)
BODY = 256
ROWS = BODY + 8
KEPT = 32
SLOTS_OUT = 144
KAPPA = math.log2(math.e) / 12.0
F32, BF16 = jnp.float32, jnp.bfloat16


def along_row(stage, step):
    pairs = []
    for x in range(4):
        for z in range(4):
            for y in range(4):
                for c in range(2):
                    if (c == 0) == (stage == 1):
                        to = ((x + step) % 4, z)
                    else:
                        to = (x, (z + step) % 4)
                    pairs.append((((x * 4 + z) * 4 + y) * 2 + c, ((to[0] * 4 + to[1]) * 4 + y) * 2 + c))
    return pairs


def hop(a, stage, step):
    return lax.ppermute(a, ALL, along_row(stage, step))


def gather_line(block):
    far = hop(block, 1, 2)
    ahead = hop(block, 1, -1)
    behind = hop(block, 1, 1)
    return block, ahead, far, behind


def gather_plane(line):
    low, high = jnp.stack(line[0:2]), jnp.stack(line[2:4])
    left_low = hop(low, 2, 1)
    right_high = hop(high, 2, -1)
    left_high = hop(high, 2, 1)
    right_low = hop(low, 2, -1)
    far_low = hop(left_low, 2, 1)
    far_high = hop(right_high, 2, -1)
    return low, high, right_low, right_high, far_low, far_high, left_low, left_high


def gather_row(block):
    return gather_plane(gather_line(block))


def swap_core(a):
    return lax.ppermute(a, C, [(0, 1), (1, 0)])


def shift_y(a, step):
    return lax.ppermute(a, Y, [(i, (i + step) % 4) for i in range(4)])


def reduce_col(keep, other):
    got = swap_core(other)
    one, two, three = [keep[j] + got[j] for j in (1, 2, 3)]
    far = shift_y(two, 2)
    return keep, got, shift_y(one, 1)[None], shift_y(three, -1)[None], far[None]


def halves(v):
    h = v.astype(BF16).astype(F32)
    m = (v - h).astype(BF16).astype(F32)
    return h, m, v - h - m


def rows_of(values, count, width):
    at = lax.broadcasted_iota(jnp.int32, (count, width), 0)
    out = jnp.zeros((count, width), F32)
    for k, value in enumerate(values):
        out = jnp.where(at == k, value, out)
    return out


def make_tile(fin, lin, fout, lout, turned, lc_ref, e_ref, pair_ref):
    h, m, l = halves(fin)
    norms = halves(-KAPPA * jnp.sum(fin * fin, axis=0, keepdims=True))
    aug = rows_of([*norms, 1.0, 1.0, 1.0, *[1.0 - lin, lin] * 3], 16, TILE)
    hm = jnp.concatenate([h, m], axis=0).T.astype(BF16)
    hl = jnp.concatenate([h, l], axis=0).T.astype(BF16)
    au = jnp.concatenate([aug, jnp.zeros((112, TILE), F32)], axis=0).T.astype(BF16)
    left = jnp.concatenate([hm, hm, hl, au], axis=1)
    g, n, k = halves(fout * (2.0 * KAPPA))
    norms = halves(-KAPPA * jnp.sum(fout * fout, axis=0, keepdims=True))
    levels = []
    for i in range(2):
        first = jnp.where(turned, lc_ref[i, 0], lc_ref[0, i])
        second = jnp.where(turned, lc_ref[i, 1], lc_ref[1, i])
        levels.append(halves(jnp.where(lout > 0.5, second, first)))
    logs = [levels[i][j] for j in range(3) for i in range(2)]
    aug = rows_of([1.0, 1.0, 1.0, *norms, *logs], 16, TILE)
    right = jnp.concatenate([g, g, n, n, k, g, aug, jnp.zeros((112, TILE), F32)], axis=0).astype(BF16)
    e_ref[...] = jnp.dot(left, right, preferred_element_type=F32)
    total = jnp.zeros((8, TILE), F32)
    for at in range(0, TILE, 64):
        t = jnp.exp2(e_ref[at : at + 64, :])
        hi = t.astype(BF16)
        pair_ref[0, at : at + 64, :] = hi
        pair_ref[1, at : at + 64, :] = (t - hi.astype(F32)).astype(BF16)
        total = total + jnp.sum(t.reshape(8, 8, TILE), axis=0)
    return jnp.sum(total, axis=0, keepdims=True)


def add_product(xs_ref, place, pair_ref, acc_ref, k):
    x = xs_ref[place]
    both = jnp.dot(x, pair_ref[0], preferred_element_type=F32)
    low = jnp.dot(x[:64], pair_ref[1], preferred_element_type=F32)
    out = both[:64] + both[64:] + low
    for g in range(4):
        acc_ref[k, g * 64 : g * 64 + 64, :] += out[:, g * 128 : g * 128 + 128]


def split_into(xs_ref, place, lanes, value):
    hi = value.astype(BF16)
    xs_ref[place, 0:64, lanes] = hi
    xs_ref[place, 64:128, lanes] = (value - hi.astype(F32)).astype(BF16)


def unpack(entry):
    return entry & 7, (entry >> 3) & 15, ((entry >> 7) & 1) == 1, entry >> 8


def first_kernel(
    own_ref, turned_ref, lc_ref, p0, p1, p2, p3, p4, p5, p6, p7, same, across,
    keep_ref, other_ref, list_ref, store_ref, facts_ref,
    fin_ref, x_ref, xs_ref, e_ref, pair_ref, acc_ref, sems, fact_sem, load_sems,
):
    loads = []
    for q, piece in enumerate((p0, p1, p2, p3, p4, p5, p6, p7)):
        at = pl.ds(2 * q, 2)
        loads.append(pltpu.make_async_copy(piece.at[:, pl.ds(0, 72), :], fin_ref.at[at], load_sems.at[q]))
        loads.append(pltpu.make_async_copy(piece.at[:, pl.ds(72, 64), :], x_ref.at[at], load_sems.at[8 + q]))
    loads.append(pltpu.make_async_copy(same.at[:, pl.ds(0, 72), :], fin_ref.at[pl.ds(16, 4)], load_sems.at[16]))
    loads.append(pltpu.make_async_copy(across.at[:, pl.ds(0, 72), :], fin_ref.at[pl.ds(20, 4)], load_sems.at[17]))
    for load in loads:
        load.start()
    acc_ref[...] = jnp.zeros_like(acc_ref)

    n = jnp.int32(0)
    for far in (False, True):
        for slot in range(8):
            list_ref[n] = own_ref[0, slot]
            n = n + own_ref[2 if far else 1, slot]
        for k in range(8):
            for there in range(16):
                place = there if k < 4 else (there & 3) * 4 + (there >> 2)
                if (place >> 2 == 2) == far:
                    list_ref[n] = k + 8 * place + 128 + 256 * (16 + k)
                    n = n + turned_ref[k, there]
        if not far:
            near = n
    list_ref[SLOTS_OUT - 2] = near
    list_ref[SLOTS_OUT - 1] = n
    for load in loads:
        load.wait()
    facts = pltpu.make_async_copy(fin_ref, facts_ref, fact_sem)
    facts.start()
    for place in range(16):
        split_into(xs_ref, place, slice(None), x_ref[place])

    def saved(t):
        slot = t & 1
        return pltpu.make_async_copy(pair_ref.at[slot], store_ref.at[jnp.minimum(t, KEPT - 1)], sems.at[slot])

    def visit(t, carry):
        k, place, turned, block = unpack(list_ref[t])
        slot = t & 1

        @pl.when((t >= 2) & (t - 2 < KEPT))
        def _():
            saved(t - 2).wait()

        pair = pair_ref.at[slot]
        sums = make_tile(
            fin_ref[place, 0:64, :], fin_ref[place, 64:65, :], fin_ref[block, 0:64, :], fin_ref[block, 64:65, :],
            turned, lc_ref, e_ref, pair,
        )

        @pl.when(t < KEPT)
        def _():
            saved(t).start()

        add_product(xs_ref, place, pair, acc_ref, k)
        spread = jnp.concatenate([sums[:, g * 128 : g * 128 + 128] for g in range(4)] + [jnp.zeros((4, 128), F32)], axis=0)
        acc_ref[k, BODY:ROWS, :] += spread
        return carry

    lax.fori_loop(0, n, visit, jnp.int32(0))
    for back in (2, 1):

        @pl.when((n >= back) & (n - back < KEPT))
        def _():
            saved(n - back).wait()

    keep_ref[...] = acc_ref[0:4]
    other_ref[...] = acc_ref[4:8]
    facts.wait()


DEPTH = 4


def products(
    first, last, local, list_ref, lc_ref, store_ref, facts_ref,
    fin_ref, fout_ref, xs_ref, e_ref, pair_ref, acc_ref, sems, fact_sems, fill,
):
    kept = jnp.clip(KEPT, first, last)

    def loaded(t):
        slot = (t - first) & (DEPTH - 1)
        return pltpu.make_async_copy(store_ref.at[jnp.minimum(t, KEPT - 1)], pair_ref.at[slot], sems.at[slot])

    for ahead in range(DEPTH):

        @pl.when(first + ahead < kept)
        def _():
            loaded(first + ahead).start()

    fill()

    def visit(t, carry):
        k, place, _, _ = unpack(list_ref[t])
        loaded(t).wait()
        add_product(xs_ref, local(place), pair_ref.at[(t - first) & (DEPTH - 1)], acc_ref, k)

        @pl.when(t + DEPTH < kept)
        def _():
            loaded(t + DEPTH).start()

        return carry

    lax.fori_loop(first, kept, visit, jnp.int32(0))

    def visit_again(t, carry):
        k, place, turned, block = unpack(list_ref[t])
        one = pltpu.make_async_copy(facts_ref.at[place], fin_ref, fact_sems.at[0])
        two = pltpu.make_async_copy(facts_ref.at[block], fout_ref, fact_sems.at[1])
        one.start()
        two.start()
        one.wait()
        two.wait()
        pair = pair_ref.at[0]
        make_tile(fin_ref[0:64, :], fin_ref[64:65, :], fout_ref[0:64, :], fout_ref[64:65, :], turned, lc_ref, e_ref, pair)
        add_product(xs_ref, local(place), pair, acc_ref, k)
        return carry

    lax.fori_loop(kept, last, visit_again, jnp.int32(0))


def fill_from(pieces, xs_ref):
    sums = jnp.zeros((8, 128), F32)
    for q, piece in enumerate(pieces):
        for j in range(2):
            for g in range(4):
                split_into(xs_ref, 2 * q + j, slice(g * 128, g * 128 + 128), piece[j, g * 64 : g * 64 + 64, :])
            sums = sums + piece[j, BODY:ROWS, :]
    return sums


def near_kernel(
    list_ref, lc_ref, p0, p1, p2, p3, p6, p7, store_ref, facts_ref, acc_ref,
    fin_ref, fout_ref, xs_ref, e_ref, pair_ref, sems, fact_sems,
):
    def fill():
        acc_ref[...] = jnp.zeros_like(acc_ref)
        sums = fill_from((p0, p1, p2, p3, p6, p7), xs_ref)
        for k in range(8):
            acc_ref[k, BODY:ROWS, :] = sums

    products(
        jnp.int32(0), list_ref[SLOTS_OUT - 2], lambda p: jnp.where(p >= 12, p - 4, p),
        list_ref, lc_ref, store_ref, facts_ref,
        fin_ref, fout_ref, xs_ref, e_ref, pair_ref, acc_ref, sems, fact_sems, fill,
    )


def far_kernel(
    list_ref, lc_ref, p4, p5, near_ref, store_ref, facts_ref, keep_ref, other_ref,
    fin_ref, fout_ref, xs_ref, e_ref, pair_ref, acc_ref, sems, fact_sems,
):
    def fill():
        acc_ref[...] = near_ref[...]
        sums = fill_from((p4, p5), xs_ref)
        for k in range(8):
            acc_ref[k, BODY:ROWS, :] += sums

    products(
        list_ref[SLOTS_OUT - 2], list_ref[SLOTS_OUT - 1], lambda p: p - 8,
        list_ref, lc_ref, store_ref, facts_ref,
        fin_ref, fout_ref, xs_ref, e_ref, pair_ref, acc_ref, sems, fact_sems, fill,
    )
    keep_ref[...] = acc_ref[0:4]
    other_ref[...] = acc_ref[4:8]


def group(g):
    return slice(g * 64, g * 64 + 64)


def lanes(g):
    return slice(g * 128, g * 128 + 128)


def sum_rows(first, second):
    both = jnp.concatenate([first, second], axis=0)
    column = jnp.broadcast_to(jnp.sum(both, axis=1, keepdims=True), (128, 128))
    return column.T[0:8, :]


def columns_of(row):
    turned = jnp.broadcast_to(row, (128, 128)).T
    return turned[0:64], turned[64:128]


def total_of(parts, rows):
    a, b, c, d, e = (part[0, rows, :] for part in parts)
    return (a + b) + (c + d) + e


def after_first(a, b, c, d, e, r_ref, err_ref, w_ref, diag_ref):
    parts = (a, b, c, d, e)
    errors = jnp.concatenate([err_ref[:, lanes(g)] for g in range(4)], axis=0)
    diag = errors + total_of(parts, slice(BODY, BODY + 4))
    diag_ref[0:4, :] = diag
    diag_ref[4:8, :] = jnp.zeros((4, 128), F32)
    rr, rw = jnp.zeros((64, 128), F32), jnp.zeros((64, 128), F32)
    for g in range(4):
        r = r_ref[:, lanes(g)]
        w = diag[g : g + 1, :] * r + total_of(parts, group(g))
        w_ref[group(g), :] = w
        rr, rw = rr + r * r, rw + r * w
    w_ref[BODY:ROWS, :] = sum_rows(rr, rw)


def after_second(a, b, c, d, e, r_ref, w_ref, diag_ref, next_ref, r1_ref, q_ref, past_ref):
    parts = (a, b, c, d, e)
    rr0, rw0 = columns_of(total_of(parts, slice(BODY, BODY + 1)))
    alpha = rr0 / rw0
    past_ref[0:64, :] = alpha
    past_ref[64:128, :] = rr0
    rr, rw = jnp.zeros((64, 128), F32), jnp.zeros((64, 128), F32)
    for g in range(4):
        w0 = w_ref[group(g), :]
        q = diag_ref[g : g + 1, :] * w0 + total_of(parts, group(g))
        r = r_ref[:, lanes(g)] - alpha * w0
        w = w0 - alpha * q
        q_ref[group(g), :] = q
        r1_ref[group(g), :] = r
        next_ref[group(g), :] = w
        rr, rw = rr + r * r, rw + r * w
    next_ref[BODY:ROWS, :] = sum_rows(rr, rw)


def after_third(
    a, b, c, d, e, r_ref, w0_ref, diag_ref, w1_ref, r1_ref, q_ref, past_ref,
    sums_ref, r2_ref, w2_ref, s1_ref, p1_ref, x_ref, now_ref,
):
    parts = (a, b, c, d, e)
    rr1, rw1 = columns_of(total_of(parts, slice(BODY, BODY + 1)))
    alpha0, rr0 = past_ref[0:64, :], past_ref[64:128, :]
    beta = rr1 / rr0
    alpha = rr1 / (rw1 - beta * rr1 / alpha0)
    now_ref[0:64, :] = alpha
    now_ref[64:128, :] = rr1
    rr, rw = jnp.zeros((64, 128), F32), jnp.zeros((64, 128), F32)
    for g in range(4):
        w1, r1, r0 = w1_ref[group(g), :], r1_ref[group(g), :], r_ref[:, lanes(g)]
        q1 = diag_ref[g : g + 1, :] * w1 + total_of(parts, group(g))
        s = w1 + beta * w0_ref[group(g), :]
        z = q1 + beta * q_ref[group(g), :]
        p = r1 + beta * r0
        r = r1 - alpha * s
        w = w1 - alpha * z
        s1_ref[group(g), :] = s
        p1_ref[group(g), :] = p
        x_ref[group(g), :] = alpha0 * r0 + alpha * p
        r2_ref[group(g), :] = r
        w2_ref[group(g), :] = w
        rr, rw = rr + r * r, rw + r * w
    sums_ref[...] = sum_rows(rr, rw)


def finish(sums_ref, r2_ref, w2_ref, s1_ref, p1_ref, x_ref, now_ref, inc_ref, res_ref):
    rr2, rw2 = columns_of(sums_ref[...])
    alpha1, rr1 = now_ref[0:64, :], now_ref[64:128, :]
    beta = rr2 / rr1
    alpha = rr2 / (rw2 - beta * rr2 / alpha1)
    for g in range(4):
        r = r2_ref[group(g), :]
        p = r + beta * p1_ref[group(g), :]
        s = w2_ref[group(g), :] + beta * s1_ref[group(g), :]
        inc_ref[:, lanes(g)] = x_ref[group(g), :] + alpha * p
        res_ref[:, lanes(g)] = r - alpha * s


VMEM = pl.BlockSpec(memory_space=pltpu.VMEM)
SMEM = pl.BlockSpec(memory_space=pltpu.SMEM)
ANY = pl.BlockSpec(memory_space=pl.ANY)


FIRST = pl.BlockSpec((1, ROWS, 128), lambda i: (0, 0, 0))


def small_call(body, shapes, args, parts=()):
    out = [jax.ShapeDtypeStruct(s, F32) for s in shapes]
    return pl.pallas_call(
        body,
        out_shape=out,
        grid=(1,),
        in_specs=[FIRST] * len(parts) + [VMEM] * len(args),
        out_specs=[VMEM] * len(shapes),
        compiler_params=pltpu.CompilerParams(vmem_limit_bytes=12 << 20),
        cost_estimate=pl.CostEstimate(flops=4_000_000, bytes_accessed=2_000_000, transcendentals=0),
    )(*parts, *args)


PART = jax.ShapeDtypeStruct((4, ROWS, 128), F32)


ACC = jax.ShapeDtypeStruct((8, ROWS, 128), F32)


def first_operate(own, turned, log_coupling, pieces, same, across):
    return pl.pallas_call(
        first_kernel,
        out_shape=[
            PART,
            PART,
            jax.ShapeDtypeStruct((SLOTS_OUT,), jnp.int32),
            jax.ShapeDtypeStruct((KEPT, 2, TILE, TILE), BF16),
            jax.ShapeDtypeStruct((24, 72, TILE), F32),
        ],
        in_specs=[SMEM, SMEM, SMEM] + [ANY] * 10,
        out_specs=[VMEM, VMEM, SMEM, ANY, ANY],
        scratch_shapes=[
            pltpu.VMEM((24, 72, TILE), F32),
            pltpu.VMEM((16, 64, TILE), F32),
            pltpu.VMEM((16, 128, TILE), BF16),
            pltpu.VMEM((TILE, TILE), F32),
            pltpu.VMEM((2, 2, TILE, TILE), BF16),
            pltpu.VMEM((8, ROWS, 128), F32),
            pltpu.SemaphoreType.DMA((2,)),
            pltpu.SemaphoreType.DMA,
            pltpu.SemaphoreType.DMA((18,)),
        ],
        compiler_params=pltpu.CompilerParams(vmem_limit_bytes=28 << 20),
        cost_estimate=pl.CostEstimate(flops=8_000_000_000, bytes_accessed=20_000_000, transcendentals=2_000_000),
    )(own, turned, log_coupling, *pieces, same, across)


def scratch(places):
    return [
        pltpu.VMEM((72, TILE), F32),
        pltpu.VMEM((72, TILE), F32),
        pltpu.VMEM((places, 128, TILE), BF16),
        pltpu.VMEM((TILE, TILE), F32),
        pltpu.VMEM((DEPTH, 2, TILE, TILE), BF16),
    ]


SEMS = [pltpu.SemaphoreType.DMA((DEPTH,)), pltpu.SemaphoreType.DMA((2,))]


def later_operate(listed, log_coupling, pieces, store, facts):
    near = pl.pallas_call(
        near_kernel,
        out_shape=ACC,
        in_specs=[SMEM, SMEM] + [VMEM] * 6 + [ANY] * 2,
        out_specs=VMEM,
        scratch_shapes=scratch(12) + SEMS,
        compiler_params=pltpu.CompilerParams(vmem_limit_bytes=24 << 20),
        cost_estimate=pl.CostEstimate(flops=3_000_000_000, bytes_accessed=12_000_000, transcendentals=0),
    )(listed, log_coupling, *pieces[0:4], *pieces[6:8], store, facts)
    return pl.pallas_call(
        far_kernel,
        out_shape=[PART, PART],
        in_specs=[SMEM, SMEM] + [VMEM] * 3 + [ANY] * 2,
        out_specs=[VMEM, VMEM],
        scratch_shapes=scratch(4) + [pltpu.VMEM((8, ROWS, 128), F32)] + SEMS,
        compiler_params=pltpu.CompilerParams(vmem_limit_bytes=24 << 20),
        cost_estimate=pl.CostEstimate(flops=1_000_000_000, bytes_accessed=6_000_000, transcendentals=0),
    )(listed, log_coupling, *pieces[4:6], near, store, facts)


def own_entries(slots, place):
    x, z, y, c = place
    a, b = slots[:, 0], slots[:, 1]
    dx, dz = ((b >> 2) - x) & 3, ((b & 3) - z) & 3
    s1, s2 = jnp.where(c == 0, dx, dz), jnp.where(c == 0, dz, dx)
    k = ((a & 1) ^ c) * 4 + (((a >> 1) - y) & 3)
    entry = k + 8 * (s2 * 4 + s1) + 256 * (16 + k)
    far = (s2 == 2).astype(jnp.int32)
    return jnp.stack([entry, slots[:, 2] * (1 - far), slots[:, 2] * far])


def to_everyone(row, count, axes):
    copies = jnp.broadcast_to(row.reshape(1, 1, 128), (count, 1, 128))
    return lax.all_to_all(copies, axes, split_axis=0, concat_axis=0, tiled=True)


def laid(parts, height, width):
    total, at = 0.0, 0
    for part in parts:
        total = total + jnp.pad(part, ((at, height - at - part.shape[0]), (0, width - part.shape[1])))
        at += part.shape[0]
    return total


def below(rows):
    padded = [jnp.pad(row, ((0, 0), (0, TILE - row.shape[1]))) for row in rows]
    return jnp.concatenate([*padded, jnp.zeros((8 - len(rows), TILE), F32)])


def shards(innovations, obs_factors, component, obs_error, coupling, tile_slots):
    place = tuple(lax.axis_index(axis) for axis in ALL)
    x, z, y, c = place
    label = component.astype(F32)[None, :]
    slots = tile_slots[0, 0]
    lane = lax.broadcasted_iota(jnp.int32, (1, 128), 1)
    cell = slots[:, 0:1] * 16 + slots[:, 1:2]
    cells = jnp.sum(jnp.where(cell == lane, slots[:, 2:3], 0), axis=0, keepdims=True).astype(F32)
    payload = jnp.concatenate([obs_factors, below([label, cells]), innovations], axis=0)
    line = gather_line(payload)
    pieces = gather_plane(line)
    cells = laid([block[65:66, 0:128] for block in line], 4, 128)
    cells = [cells, hop(cells, 2, -1), hop(cells, 2, 2), hop(cells, 2, 1)]
    facts = laid([obs_factors, below([label]), *cells], 88, TILE)
    same = jnp.stack([facts, shift_y(facts, -1), shift_y(facts, 2), shift_y(facts, 1)])
    across = swap_core(same)
    mine = (lane == (y * 2 + c) * 16 + x * 4 + z).astype(F32)
    seen = [jnp.sum(facts[:, 72:88, 0:128] * mine[None], axis=2) for facts in (same, across)]
    turned = (jnp.concatenate(seen) > 0.5).astype(jnp.int32)
    own = own_entries(slots, place)
    log_coupling = jnp.log2(coupling)
    error_row = obs_error[None, :]

    vec, body, two = (ROWS, 128), (BODY, 128), (128, 128)
    keep, other, listed, store, kept_facts = first_operate(own, turned, log_coupling, pieces, same, across)
    parts = reduce_col(keep, other)
    w0, diag = small_call(after_first, [vec, (8, 128)], (innovations, error_row), parts)

    keep, other = later_operate(listed, log_coupling, gather_row(w0), store, kept_facts)
    parts = reduce_col(keep, other)
    w1, r1, q0, past = small_call(after_second, [vec, body, body, two], (innovations, w0, diag), parts)

    keep, other = later_operate(listed, log_coupling, gather_row(w1), store, kept_facts)
    parts = reduce_col(keep, other)
    sums, r2, w2, s1, p1, x2, now = small_call(
        after_third,
        [(8, 128), body, body, body, body, body, two],
        (innovations, w0, diag, w1, r1, q0, past),
        parts,
    )
    sums = jnp.sum(to_everyone(sums[0:1], 128, ALL), axis=0)
    increment, residual = small_call(finish, [(64, TILE)] * 2, (sums, r2, w2, s1, p1, x2, now))
    return increment, residual


def solution(mesh):
    finer = Mesh(mesh.devices.reshape(4, 4, 4, 2), ALL)
    in_specs = (P(None, ALL), P(None, ALL), P(ALL), P(ALL), P(), P(ROW, COL, None, None))
    out_specs = (P(None, ALL), P(None, ALL))
    return jax.shard_map(shards, mesh=finer, in_specs=in_specs, out_specs=out_specs, check_vma=False)
```

```python
import functools
import math

import jax
import jax.numpy as jnp
from jax import lax
from jax.experimental import pallas as pl
from jax.experimental.pallas import tpu as pltpu
from jax.sharding import Mesh
from jax.sharding import PartitionSpec as P

TILE = 512
X, Z, Y, C = "row_0", "row_1", "col_0", "col_1"
ALL = (X, Z, Y, C)
ROW, COL = (X, Z), (Y, C)
BODY = 256
ROWS = BODY + 8
KEPT = 48
SLOTS_OUT = 144
KAPPA = math.log2(math.e) / 12.0
F32, BF16 = jnp.float32, jnp.bfloat16


def along_row(stage, step):
    pairs = []
    for x in range(4):
        for z in range(4):
            for y in range(4):
                for c in range(2):
                    if (c == 0) == (stage == 1):
                        to = ((x + step) % 4, z)
                    else:
                        to = (x, (z + step) % 4)
                    pairs.append((((x * 4 + z) * 4 + y) * 2 + c, ((to[0] * 4 + to[1]) * 4 + y) * 2 + c))
    return pairs


def hop(a, stage, step):
    return lax.ppermute(a, ALL, along_row(stage, step))


def gather_line(block):
    far = hop(block, 1, 2)
    ahead = hop(block, 1, -1)
    behind = hop(block, 1, 1)
    return block, ahead, far, behind


def gather_plane(line):
    low, high = jnp.stack(line[0:2]), jnp.stack(line[2:4])
    left_low = hop(low, 2, 1)
    right_high = hop(high, 2, -1)
    left_high = hop(high, 2, 1)
    right_low = hop(low, 2, -1)
    far_low = hop(left_low, 2, 1)
    far_high = hop(right_high, 2, -1)
    return low, high, right_low, right_high, far_low, far_high, left_low, left_high


def gather_row(block):
    return gather_plane(gather_line(block))


def swap_core(a):
    return lax.ppermute(a, C, [(0, 1), (1, 0)])


def shift_y(a, step):
    return lax.ppermute(a, Y, [(i, (i + step) % 4) for i in range(4)])


def reduce_col(keep, other):
    got = swap_core(other)
    one, two, three = [keep[j] + got[j] for j in (1, 2, 3)]
    far = shift_y(two, 2)
    return keep, got, shift_y(one, 1)[None], shift_y(three, -1)[None], far[None]


def halves(v):
    h = v.astype(BF16).astype(F32)
    m = (v - h).astype(BF16).astype(F32)
    return h, m, v - h - m


def rows_of(values, count, width):
    at = lax.broadcasted_iota(jnp.int32, (count, width), 0)
    out = jnp.zeros((count, width), F32)
    for k, value in enumerate(values):
        out = jnp.where(at == k, value, out)
    return out


def make_tile(fin, lin, fout, lout, turned, lc_ref, e_ref, pair_ref):
    h, m, l = halves(fin)
    norms = halves(-KAPPA * jnp.sum(fin * fin, axis=0, keepdims=True))
    aug = rows_of([*norms, 1.0, 1.0, 1.0, *[1.0 - lin, lin] * 3], 16, TILE)
    hm = jnp.concatenate([h, m], axis=0).T.astype(BF16)
    hl = jnp.concatenate([h, l], axis=0).T.astype(BF16)
    au = jnp.concatenate([aug, jnp.zeros((112, TILE), F32)], axis=0).T.astype(BF16)
    left = jnp.concatenate([hm, hm, hl, au], axis=1)
    g, n, k = halves(fout * (2.0 * KAPPA))
    norms = halves(-KAPPA * jnp.sum(fout * fout, axis=0, keepdims=True))
    levels = []
    for i in range(2):
        first = jnp.where(turned, lc_ref[i, 0], lc_ref[0, i])
        second = jnp.where(turned, lc_ref[i, 1], lc_ref[1, i])
        levels.append(halves(jnp.where(lout > 0.5, second, first)))
    logs = [levels[i][j] for j in range(3) for i in range(2)]
    aug = rows_of([1.0, 1.0, 1.0, *norms, *logs], 16, TILE)
    right = jnp.concatenate([g, g, n, n, k, g, aug, jnp.zeros((112, TILE), F32)], axis=0).astype(BF16)
    e_ref[...] = jnp.dot(left, right, preferred_element_type=F32)
    total = jnp.zeros((8, TILE), F32)
    for at in range(0, TILE, 64):
        t = jnp.exp2(e_ref[at : at + 64, :])
        hi = t.astype(BF16)
        pair_ref[0, at : at + 64, :] = hi
        pair_ref[1, at : at + 64, :] = (t - hi.astype(F32)).astype(BF16)
        total = total + jnp.sum(t.reshape(8, 8, TILE), axis=0)
    return jnp.sum(total, axis=0, keepdims=True)


def add_product(xs_ref, place, pair_ref, acc_ref, k):
    x = xs_ref[place]
    both = jnp.dot(x, pair_ref[0], preferred_element_type=F32)
    low = jnp.dot(x[:64], pair_ref[1], preferred_element_type=F32)
    out = both[:64] + both[64:] + low
    for g in range(4):
        acc_ref[k, g * 64 : g * 64 + 64, :] += out[:, g * 128 : g * 128 + 128]


def split_into(xs_ref, place, lanes, value):
    hi = value.astype(BF16)
    xs_ref[place, 0:64, lanes] = hi
    xs_ref[place, 64:128, lanes] = (value - hi.astype(F32)).astype(BF16)


def unpack(entry):
    return entry & 7, (entry >> 3) & 15, ((entry >> 7) & 1) == 1, entry >> 8


def first_kernel(
    place_ref, slots_ref, lc_ref, p0, p1, p2, p3, p4, p5, p6, p7, cells, same, across,
    keep_ref, other_ref, list_ref, store_ref, facts_ref,
    fin_ref, x_ref, xs_ref, cells_ref, hits_ref, hit_ref, e_ref, pair_ref, acc_ref, fact_sem, load_sems, save_sems,
):
    loads = []
    for q, piece in enumerate((p0, p1, p2, p3, p4, p5, p6, p7)):
        at = pl.ds(2 * q, 2)
        loads.append(pltpu.make_async_copy(piece.at[:, pl.ds(0, 72), :], fin_ref.at[at], load_sems.at[8 + q]))
        loads.append(pltpu.make_async_copy(piece.at[:, pl.ds(72, 64), :], x_ref.at[at], load_sems.at[16 + q]))
    loads.append(pltpu.make_async_copy(same, fin_ref.at[pl.ds(16, 4)], load_sems.at[24]))
    loads.append(pltpu.make_async_copy(across, fin_ref.at[pl.ds(20, 4)], load_sems.at[25]))
    x, z, y, c = (place_ref[axis] for axis in range(4))
    for place in range(16):
        s1, s2 = place & 3, place >> 2
        dx, dz = jnp.where(c == 0, s1, s2), jnp.where(c == 0, s2, s1)
        row = ((x + dx) & 3) * 4 + ((z + dz) & 3)
        loads.append(pltpu.make_async_copy(cells.at[row], cells_ref.at[pl.ds(8 * place, 8)], load_sems.at[26 + place]))
    for load in loads:
        load.start()
    acc_ref[...] = jnp.zeros_like(acc_ref)
    for load in loads[18:34]:
        load.wait()
    mine = lax.broadcasted_iota(jnp.int32, (128, 128), 1) == (y * 2 + c) * 16 + x * 4 + z
    found = jnp.where(mine, cells_ref[...], 0.0)
    found = jnp.broadcast_to(jnp.sum(found, axis=1, keepdims=True), (128, 128))
    hits_ref[...] = found.T[0:8, :].astype(jnp.int32)
    hits = pltpu.make_async_copy(hits_ref, hit_ref, fact_sem)
    hits.start()
    own = []
    for slot in range(8):
        a, b, live = (slots_ref[0, 0, slot, field] for field in range(3))
        dx, dz = ((b >> 2) - x) & 3, ((b & 3) - z) & 3
        s1, s2 = jnp.where(c == 0, dx, dz), jnp.where(c == 0, dz, dx)
        k = ((a & 1) ^ c) * 4 + (((a >> 1) - y) & 3)
        own.append((k + 8 * (s2 * 4 + s1) + 256 * (16 + k), live, jnp.where(s2 == 2, 1, 0)))
    hits.wait()
    n = jnp.int32(0)
    for far in (False, True):
        for entry, live, there in own:
            list_ref[n] = entry
            n = n + live * (there if far else 1 - there)
        for place in range(8, 12) if far else (*range(8), *range(12, 16)):
            for k in range(8):
                list_ref[n] = k + 8 * place + 128 + 256 * (16 + k)
                n = n + hit_ref[0, place * 8 + k]
        if not far:
            near = n
    list_ref[SLOTS_OUT - 2] = near
    list_ref[SLOTS_OUT - 1] = n
    for load in loads[0:18]:
        load.wait()
    facts = pltpu.make_async_copy(fin_ref, facts_ref, fact_sem)
    facts.start()
    for place in range(16):
        split_into(xs_ref, place, slice(None), x_ref[place])

    def saved(t):
        slot = t & 1
        return pltpu.make_async_copy(pair_ref.at[slot], store_ref.at[jnp.minimum(t, KEPT - 1)], save_sems.at[slot])

    def visit(t, carry):
        k, place, turned, block = unpack(list_ref[t])
        slot = t & 1

        @pl.when((t >= 2) & (t - 2 < KEPT))
        def _():
            saved(t - 2).wait()

        pair = pair_ref.at[slot]
        sums = make_tile(
            fin_ref[place, 0:64, :], fin_ref[place, 64:65, :], fin_ref[block, 0:64, :], fin_ref[block, 64:65, :],
            turned, lc_ref, e_ref, pair,
        )

        @pl.when(t < KEPT)
        def _():
            saved(t).start()

        add_product(xs_ref, place, pair, acc_ref, k)
        spread = jnp.concatenate([sums[:, g * 128 : g * 128 + 128] for g in range(4)] + [jnp.zeros((4, 128), F32)], axis=0)
        acc_ref[k, BODY:ROWS, :] += spread
        return carry

    lax.fori_loop(0, n, visit, jnp.int32(0))
    for back in (2, 1):

        @pl.when((n >= back) & (n - back < KEPT))
        def _():
            saved(n - back).wait()

    keep_ref[...] = acc_ref[0:4]
    other_ref[...] = acc_ref[4:8]
    facts.wait()


DEPTH = 4


def products(
    first, last, local, list_ref, lc_ref, store_ref, facts_ref,
    fin_ref, fout_ref, xs_ref, e_ref, pair_ref, acc_ref, sems, fact_sems, fill,
):
    kept = jnp.clip(KEPT, first, last)

    def loaded(t):
        slot = (t - first) & (DEPTH - 1)
        return pltpu.make_async_copy(store_ref.at[jnp.minimum(t, KEPT - 1)], pair_ref.at[slot], sems.at[slot])

    for ahead in range(DEPTH):

        @pl.when(first + ahead < kept)
        def _():
            loaded(first + ahead).start()

    fill()

    def visit(t, carry):
        k, place, _, _ = unpack(list_ref[t])
        loaded(t).wait()
        add_product(xs_ref, local(place), pair_ref.at[(t - first) & (DEPTH - 1)], acc_ref, k)

        @pl.when(t + DEPTH < kept)
        def _():
            loaded(t + DEPTH).start()

        return carry

    lax.fori_loop(first, kept, visit, jnp.int32(0))

    def visit_again(t, carry):
        k, place, turned, block = unpack(list_ref[t])
        one = pltpu.make_async_copy(facts_ref.at[place], fin_ref, fact_sems.at[0])
        two = pltpu.make_async_copy(facts_ref.at[block], fout_ref, fact_sems.at[1])
        one.start()
        two.start()
        one.wait()
        two.wait()
        pair = pair_ref.at[0]
        make_tile(fin_ref[0:64, :], fin_ref[64:65, :], fout_ref[0:64, :], fout_ref[64:65, :], turned, lc_ref, e_ref, pair)
        add_product(xs_ref, local(place), pair, acc_ref, k)
        return carry

    lax.fori_loop(kept, last, visit_again, jnp.int32(0))


def fill_from(pieces, xs_ref):
    sums = jnp.zeros((8, 128), F32)
    for q, piece in enumerate(pieces):
        for j in range(2):
            for g in range(4):
                split_into(xs_ref, 2 * q + j, slice(g * 128, g * 128 + 128), piece[j, g * 64 : g * 64 + 64, :])
            sums = sums + piece[j, BODY:ROWS, :]
    return sums


def near_kernel(
    list_ref, lc_ref, p0, p1, p2, p3, p6, p7, store_ref, facts_ref, acc_ref,
    fin_ref, fout_ref, xs_ref, e_ref, pair_ref, sems, fact_sems,
):
    def fill():
        acc_ref[...] = jnp.zeros_like(acc_ref)
        sums = fill_from((p0, p1, p2, p3, p6, p7), xs_ref)
        for k in range(8):
            acc_ref[k, BODY:ROWS, :] = sums

    products(
        jnp.int32(0), list_ref[SLOTS_OUT - 2], lambda p: jnp.where(p >= 12, p - 4, p),
        list_ref, lc_ref, store_ref, facts_ref,
        fin_ref, fout_ref, xs_ref, e_ref, pair_ref, acc_ref, sems, fact_sems, fill,
    )


def far_kernel(
    list_ref, lc_ref, p4, p5, near_ref, store_ref, facts_ref, keep_ref, other_ref,
    fin_ref, fout_ref, xs_ref, e_ref, pair_ref, acc_ref, sems, fact_sems,
):
    def fill():
        acc_ref[...] = near_ref[...]
        sums = fill_from((p4, p5), xs_ref)
        for k in range(8):
            acc_ref[k, BODY:ROWS, :] += sums

    products(
        list_ref[SLOTS_OUT - 2], list_ref[SLOTS_OUT - 1], lambda p: p - 8,
        list_ref, lc_ref, store_ref, facts_ref,
        fin_ref, fout_ref, xs_ref, e_ref, pair_ref, acc_ref, sems, fact_sems, fill,
    )
    keep_ref[...] = acc_ref[0:4]
    other_ref[...] = acc_ref[4:8]


def group(g):
    return slice(g * 64, g * 64 + 64)


def lanes(g):
    return slice(g * 128, g * 128 + 128)


def sum_rows(first, second):
    both = jnp.concatenate([first, second], axis=0)
    column = jnp.broadcast_to(jnp.sum(both, axis=1, keepdims=True), (128, 128))
    return column.T[0:8, :]


def columns_of(row):
    turned = jnp.broadcast_to(row, (128, 128)).T
    return turned[0:64], turned[64:128]


def total_of(parts, rows):
    a, b, c, d, e = (part[0, rows, :] for part in parts)
    return (a + b) + (c + d) + e


def after_first(a, b, c, d, e, r_ref, err_ref, w_ref, diag_ref):
    parts = (a, b, c, d, e)
    errors = jnp.concatenate([err_ref[:, lanes(g)] for g in range(4)], axis=0)
    diag = errors + total_of(parts, slice(BODY, BODY + 4))
    diag_ref[0:4, :] = diag
    diag_ref[4:8, :] = jnp.zeros((4, 128), F32)
    rr, rw = jnp.zeros((64, 128), F32), jnp.zeros((64, 128), F32)
    for g in range(4):
        r = r_ref[:, lanes(g)]
        w = diag[g : g + 1, :] * r + total_of(parts, group(g))
        w_ref[group(g), :] = w
        rr, rw = rr + r * r, rw + r * w
    w_ref[BODY:ROWS, :] = sum_rows(rr, rw)


def after_second(a, b, c, d, e, r_ref, w_ref, diag_ref, next_ref, r1_ref, q_ref, past_ref):
    parts = (a, b, c, d, e)
    rr0, rw0 = columns_of(total_of(parts, slice(BODY, BODY + 1)))
    alpha = rr0 / rw0
    past_ref[0:64, :] = alpha
    past_ref[64:128, :] = rr0
    rr, rw = jnp.zeros((64, 128), F32), jnp.zeros((64, 128), F32)
    for g in range(4):
        w0 = w_ref[group(g), :]
        q = diag_ref[g : g + 1, :] * w0 + total_of(parts, group(g))
        r = r_ref[:, lanes(g)] - alpha * w0
        w = w0 - alpha * q
        q_ref[group(g), :] = q
        r1_ref[group(g), :] = r
        next_ref[group(g), :] = w
        rr, rw = rr + r * r, rw + r * w
    next_ref[BODY:ROWS, :] = sum_rows(rr, rw)


def after_third(
    a, b, c, d, e, r_ref, w0_ref, diag_ref, w1_ref, r1_ref, q_ref, past_ref,
    sums_ref, r2_ref, w2_ref, s1_ref, p1_ref, x_ref, now_ref,
):
    parts = (a, b, c, d, e)
    rr1, rw1 = columns_of(total_of(parts, slice(BODY, BODY + 1)))
    alpha0, rr0 = past_ref[0:64, :], past_ref[64:128, :]
    beta = rr1 / rr0
    alpha = rr1 / (rw1 - beta * rr1 / alpha0)
    now_ref[0:64, :] = alpha
    now_ref[64:128, :] = rr1
    rr, rw = jnp.zeros((64, 128), F32), jnp.zeros((64, 128), F32)
    for g in range(4):
        w1, r1, r0 = w1_ref[group(g), :], r1_ref[group(g), :], r_ref[:, lanes(g)]
        q1 = diag_ref[g : g + 1, :] * w1 + total_of(parts, group(g))
        s = w1 + beta * w0_ref[group(g), :]
        z = q1 + beta * q_ref[group(g), :]
        p = r1 + beta * r0
        r = r1 - alpha * s
        w = w1 - alpha * z
        s1_ref[group(g), :] = s
        p1_ref[group(g), :] = p
        x_ref[group(g), :] = alpha0 * r0 + alpha * p
        r2_ref[group(g), :] = r
        w2_ref[group(g), :] = w
        rr, rw = rr + r * r, rw + r * w
    sums_ref[...] = sum_rows(rr, rw)


def finish(sums_ref, r2_ref, w2_ref, s1_ref, p1_ref, x_ref, now_ref, inc_ref, res_ref):
    rr2, rw2 = columns_of(sums_ref[...])
    alpha1, rr1 = now_ref[0:64, :], now_ref[64:128, :]
    beta = rr2 / rr1
    alpha = rr2 / (rw2 - beta * rr2 / alpha1)
    for g in range(4):
        r = r2_ref[group(g), :]
        p = r + beta * p1_ref[group(g), :]
        s = w2_ref[group(g), :] + beta * s1_ref[group(g), :]
        inc_ref[:, lanes(g)] = x_ref[group(g), :] + alpha * p
        res_ref[:, lanes(g)] = r - alpha * s


def pack_kernel(slots_ref, factors_ref, component_ref, values_ref, out_ref, facts_ref, label_ref, sems):
    loads = [
        pltpu.make_async_copy(component_ref, label_ref, sems.at[0]),
        pltpu.make_async_copy(factors_ref, out_ref.at[pl.ds(0, 64), :], sems.at[1]),
        pltpu.make_async_copy(values_ref, out_ref.at[pl.ds(72, 64), :], sems.at[2]),
    ]
    for load in loads:
        load.start()
    lane = lax.broadcasted_iota(jnp.int32, (8, TILE), 1)
    row = lax.broadcasted_iota(jnp.int32, (8, TILE), 0)
    cells = jnp.zeros((8, TILE), jnp.int32)
    for slot in range(8):
        cell = slots_ref[0, 0, slot, 0] * 16 + slots_ref[0, 0, slot, 1]
        cells = cells + jnp.where(lane == cell, slots_ref[0, 0, slot, 2], 0)
    for load in loads:
        load.wait()
    below = jnp.where(row == 0, label_ref[...], jnp.where(row == 1, cells, 0)).astype(F32)
    out_ref[64:72, :] = below
    facts_ref[0:64, :] = out_ref[0:64, :]
    facts_ref[64:72, :] = below


VMEM = pl.BlockSpec(memory_space=pltpu.VMEM)
SMEM = pl.BlockSpec(memory_space=pltpu.SMEM)
ANY = pl.BlockSpec(memory_space=pl.ANY)


FIRST = pl.BlockSpec((1, ROWS, 128), lambda i: (0, 0, 0))


def small_call(body, shapes, args, parts=()):
    out = [jax.ShapeDtypeStruct(s, F32) for s in shapes]
    return pl.pallas_call(
        body,
        out_shape=out,
        grid=(1,),
        in_specs=[FIRST] * len(parts) + [VMEM] * len(args),
        out_specs=[VMEM] * len(shapes),
        compiler_params=pltpu.CompilerParams(vmem_limit_bytes=12 << 20),
        cost_estimate=pl.CostEstimate(flops=4_000_000, bytes_accessed=2_000_000, transcendentals=0),
    )(*parts, *args)


def pack(slots, factors, component, values):
    return pl.pallas_call(
        pack_kernel,
        out_shape=[jax.ShapeDtypeStruct((136, TILE), F32), jax.ShapeDtypeStruct((72, TILE), F32)],
        in_specs=[SMEM, ANY, ANY, ANY],
        out_specs=[VMEM, VMEM],
        scratch_shapes=[pltpu.VMEM((1, TILE), jnp.int32), pltpu.SemaphoreType.DMA((3,))],
        compiler_params=pltpu.CompilerParams(vmem_limit_bytes=4 << 20),
    )(slots, factors, component, values)


def laid(parts):
    height, total = parts[0].shape[0], 0.0
    for k, part in enumerate(parts):
        total = total + jnp.pad(part, ((k * height, (len(parts) - 1 - k) * height), (0, 0)))
    return total


PART = jax.ShapeDtypeStruct((4, ROWS, 128), F32)


ACC = jax.ShapeDtypeStruct((8, ROWS, 128), F32)


STORE = jax.ShapeDtypeStruct((KEPT, 2, TILE, TILE), BF16)


def first_operate(place, slots, log_coupling, pieces, cells, same, across):
    return pl.pallas_call(
        first_kernel,
        out_shape=[
            PART,
            PART,
            jax.ShapeDtypeStruct((SLOTS_OUT,), jnp.int32),
            STORE,
            jax.ShapeDtypeStruct((24, 72, TILE), F32),
        ],
        in_specs=[SMEM] * 3 + [ANY] * 11,
        out_specs=[VMEM, VMEM, SMEM, ANY, ANY],
        scratch_shapes=[
            pltpu.VMEM((24, 72, TILE), F32),
            pltpu.VMEM((16, 64, TILE), F32),
            pltpu.VMEM((16, 128, TILE), BF16),
            pltpu.VMEM((128, 128), F32),
            pltpu.VMEM((8, 128), jnp.int32),
            pltpu.SMEM((8, 128), jnp.int32),
            pltpu.VMEM((TILE, TILE), F32),
            pltpu.VMEM((2, 2, TILE, TILE), BF16),
            pltpu.VMEM((8, ROWS, 128), F32),
            pltpu.SemaphoreType.DMA,
            pltpu.SemaphoreType.DMA((42,)),
            pltpu.SemaphoreType.DMA((2,)),
        ],
        compiler_params=pltpu.CompilerParams(vmem_limit_bytes=18 << 20),
        cost_estimate=pl.CostEstimate(flops=8_000_000_000, bytes_accessed=20_000_000, transcendentals=2_000_000),
    )(place, slots, log_coupling, *pieces, cells, same, across)


def scratch(places):
    return [
        pltpu.VMEM((72, TILE), F32),
        pltpu.VMEM((72, TILE), F32),
        pltpu.VMEM((places, 128, TILE), BF16),
        pltpu.VMEM((TILE, TILE), F32),
        pltpu.VMEM((DEPTH, 2, TILE, TILE), BF16),
    ]


SEMS = [pltpu.SemaphoreType.DMA((DEPTH,)), pltpu.SemaphoreType.DMA((2,))]


def later_operate(listed, log_coupling, pieces, store, facts):
    near = pl.pallas_call(
        near_kernel,
        out_shape=ACC,
        in_specs=[SMEM, SMEM] + [VMEM] * 6 + [ANY] * 2,
        out_specs=VMEM,
        scratch_shapes=scratch(12) + SEMS,
        compiler_params=pltpu.CompilerParams(vmem_limit_bytes=14 << 20),
        cost_estimate=pl.CostEstimate(flops=3_000_000_000, bytes_accessed=12_000_000, transcendentals=0),
    )(listed, log_coupling, *pieces[0:4], *pieces[6:8], store, facts)
    return pl.pallas_call(
        far_kernel,
        out_shape=[PART, PART],
        in_specs=[SMEM, SMEM] + [VMEM] * 3 + [ANY] * 2,
        out_specs=[VMEM, VMEM],
        scratch_shapes=scratch(4) + [pltpu.VMEM((8, ROWS, 128), F32)] + SEMS,
        compiler_params=pltpu.CompilerParams(vmem_limit_bytes=14 << 20),
        cost_estimate=pl.CostEstimate(flops=1_000_000_000, bytes_accessed=6_000_000, transcendentals=0),
    )(listed, log_coupling, *pieces[4:6], near, store, facts)


def to_everyone(row, count, axes):
    copies = jnp.broadcast_to(row.reshape(1, 1, 128), (count, 1, 128))
    return lax.all_to_all(copies, axes, split_axis=0, concat_axis=0, tiled=True)


def shards(innovations, obs_factors, component, obs_error, coupling, tile_slots):
    place = jnp.stack([lax.axis_index(axis) for axis in ALL]).astype(jnp.int32)
    payload, facts = pack(tile_slots, obs_factors, component[None, :], innovations)
    same = jnp.stack([facts, shift_y(facts, -1), shift_y(facts, 2), shift_y(facts, 1)])
    across = swap_core(same)
    pieces = gather_row(payload)
    cells = laid([part[k, 65:66, 0:128] for part in (same, across) for k in range(4)])
    cells = jnp.broadcast_to(cells[None], (16, 8, 128))
    cells = lax.all_to_all(cells, ROW, split_axis=0, concat_axis=0, tiled=True)
    log_coupling = jnp.log2(coupling)
    error_row = obs_error[None, :]

    vec, body, two = (ROWS, 128), (BODY, 128), (128, 128)
    keep, other, listed, store, kept_facts = first_operate(place, tile_slots, log_coupling, pieces, cells, same, across)
    parts = reduce_col(keep, other)
    w0, diag = small_call(after_first, [vec, (8, 128)], (innovations, error_row), parts)

    keep, other = later_operate(listed, log_coupling, gather_row(w0), store, kept_facts)
    parts = reduce_col(keep, other)
    w1, r1, q0, past = small_call(after_second, [vec, body, body, two], (innovations, w0, diag), parts)

    keep, other = later_operate(listed, log_coupling, gather_row(w1), store, kept_facts)
    parts = reduce_col(keep, other)
    sums, r2, w2, s1, p1, x2, now = small_call(
        after_third,
        [(8, 128), body, body, body, body, body, two],
        (innovations, w0, diag, w1, r1, q0, past),
        parts,
    )
    sums = jnp.sum(to_everyone(sums[0:1], 128, ALL), axis=0)
    increment, residual = small_call(finish, [(64, TILE)] * 2, (sums, r2, w2, s1, p1, x2, now))
    return increment, residual


def solution(mesh):
    finer = Mesh(mesh.devices.reshape(4, 4, 4, 2), ALL)
    in_specs = (P(None, ALL), P(None, ALL), P(ALL), P(ALL), P(), P(ROW, COL, None, None))
    out_specs = (P(None, ALL), P(None, ALL))
    return jax.shard_map(shards, mesh=finer, in_specs=in_specs, out_specs=out_specs, check_vma=False)
```

```python
import functools
import math

import jax
import jax.numpy as jnp
from jax import lax
from jax.experimental import pallas as pl
from jax.experimental.pallas import tpu as pltpu
from jax.sharding import Mesh
from jax.sharding import PartitionSpec as P

TILE = 512
X, Z, Y, C = "row_0", "row_1", "col_0", "col_1"
ALL = (X, Z, Y, C)
ROW, COL = (X, Z), (Y, C)
BODY = 256
ROWS = BODY + 8
KEPT = 48
SLOTS_OUT = 144
KAPPA = math.log2(math.e) / 12.0
F32, BF16 = jnp.float32, jnp.bfloat16


def along_row(stage, step):
    pairs = []
    for x in range(4):
        for z in range(4):
            for y in range(4):
                for c in range(2):
                    if (c == 0) == (stage == 1):
                        to = ((x + step) % 4, z)
                    else:
                        to = (x, (z + step) % 4)
                    pairs.append((((x * 4 + z) * 4 + y) * 2 + c, ((to[0] * 4 + to[1]) * 4 + y) * 2 + c))
    return pairs


def hop(a, stage, step):
    return lax.ppermute(a, ALL, along_row(stage, step))


def gather_line(block):
    far = hop(block, 1, 2)
    ahead = hop(block, 1, -1)
    behind = hop(block, 1, 1)
    return block, ahead, far, behind


def gather_plane(line):
    low, high = jnp.stack(line[0:2]), jnp.stack(line[2:4])
    left_low = hop(low, 2, 1)
    right_high = hop(high, 2, -1)
    left_high = hop(high, 2, 1)
    right_low = hop(low, 2, -1)
    far_low = hop(left_low, 2, 1)
    far_high = hop(right_high, 2, -1)
    return low, high, right_low, right_high, far_low, far_high, left_low, left_high


def gather_row(block):
    return gather_plane(gather_line(block))


def swap_core(a):
    return lax.ppermute(a, C, [(0, 1), (1, 0)])


def shift_y(a, step):
    return lax.ppermute(a, Y, [(i, (i + step) % 4) for i in range(4)])


def reduce_col(keep, other):
    got = swap_core(other)
    one, two, three = [keep[j] + got[j] for j in (1, 2, 3)]
    far = shift_y(two, 2)
    return keep, got, shift_y(one, 1)[None], shift_y(three, -1)[None], far[None]


def halves(v):
    h = v.astype(BF16).astype(F32)
    m = (v - h).astype(BF16).astype(F32)
    return h, m, v - h - m


def rows_of(values, count, width):
    at = lax.broadcasted_iota(jnp.int32, (count, width), 0)
    out = jnp.zeros((count, width), F32)
    for k, value in enumerate(values):
        out = jnp.where(at == k, value, out)
    return out


def make_tile(fin, lin, fout, lout, turned, lc_ref, e_ref, pair_ref):
    h, m, l = halves(fin)
    norms = halves(-KAPPA * jnp.sum(fin * fin, axis=0, keepdims=True))
    aug = rows_of([*norms, 1.0, 1.0, 1.0, *[1.0 - lin, lin] * 3], 16, TILE)
    hm = jnp.concatenate([h, m], axis=0).T.astype(BF16)
    hl = jnp.concatenate([h, l], axis=0).T.astype(BF16)
    au = jnp.concatenate([aug, jnp.zeros((112, TILE), F32)], axis=0).T.astype(BF16)
    left = jnp.concatenate([hm, hm, hl, au], axis=1)
    g, n, k = halves(fout * (2.0 * KAPPA))
    norms = halves(-KAPPA * jnp.sum(fout * fout, axis=0, keepdims=True))
    levels = []
    for i in range(2):
        first = jnp.where(turned, lc_ref[i, 0], lc_ref[0, i])
        second = jnp.where(turned, lc_ref[i, 1], lc_ref[1, i])
        levels.append(halves(jnp.where(lout > 0.5, second, first)))
    logs = [levels[i][j] for j in range(3) for i in range(2)]
    aug = rows_of([1.0, 1.0, 1.0, *norms, *logs], 16, TILE)
    right = jnp.concatenate([g, g, n, n, k, g, aug, jnp.zeros((112, TILE), F32)], axis=0).astype(BF16)
    e_ref[...] = jnp.dot(left, right, preferred_element_type=F32)
    total = jnp.zeros((8, TILE), F32)
    for at in range(0, TILE, 64):
        t = jnp.exp2(e_ref[at : at + 64, :])
        hi = t.astype(BF16)
        pair_ref[0, at : at + 64, :] = hi
        pair_ref[1, at : at + 64, :] = (t - hi.astype(F32)).astype(BF16)
        total = total + jnp.sum(t.reshape(8, 8, TILE), axis=0)
    return jnp.sum(total, axis=0, keepdims=True)


def add_product(xs_ref, place, pair_ref, acc_ref, k):
    x = xs_ref[place]
    both = jnp.dot(x, pair_ref[0], preferred_element_type=F32)
    low = jnp.dot(x[:64], pair_ref[1], preferred_element_type=F32)
    out = both[:64] + both[64:] + low
    for g in range(4):
        acc_ref[k, g * 64 : g * 64 + 64, :] += out[:, g * 128 : g * 128 + 128]


def split_into(xs_ref, place, lanes, value):
    hi = value.astype(BF16)
    xs_ref[place, 0:64, lanes] = hi
    xs_ref[place, 64:128, lanes] = (value - hi.astype(F32)).astype(BF16)


def unpack(entry):
    return entry & 7, (entry >> 3) & 15, ((entry >> 7) & 1) == 1, entry >> 8


def first_kernel(
    place_ref, slots_ref, lc_ref, p0, p1, p2, p3, p4, p5, p6, p7, cells, same, across,
    keep_ref, other_ref, list_ref, store_ref, facts_ref,
    fin_ref, x_ref, xs_ref, cells_ref, hits_ref, hit_ref, e_ref, pair_ref, acc_ref, fact_sem, load_sems, save_sems,
):
    loads = []
    for q, piece in enumerate((p0, p1, p2, p3, p4, p5, p6, p7)):
        at = pl.ds(2 * q, 2)
        loads.append(pltpu.make_async_copy(piece.at[:, pl.ds(0, 72), :], fin_ref.at[at], load_sems.at[8 + q]))
        loads.append(pltpu.make_async_copy(piece.at[:, pl.ds(72, 64), :], x_ref.at[at], load_sems.at[16 + q]))
    loads.append(pltpu.make_async_copy(same, fin_ref.at[pl.ds(16, 4)], load_sems.at[24]))
    loads.append(pltpu.make_async_copy(across, fin_ref.at[pl.ds(20, 4)], load_sems.at[25]))
    x, z, y, c = (place_ref[axis] for axis in range(4))
    for place in range(16):
        s1, s2 = place & 3, place >> 2
        dx, dz = jnp.where(c == 0, s1, s2), jnp.where(c == 0, s2, s1)
        row = ((x + dx) & 3) * 4 + ((z + dz) & 3)
        loads.append(pltpu.make_async_copy(cells.at[row], cells_ref.at[pl.ds(8 * place, 8)], load_sems.at[26 + place]))
    for load in loads:
        load.start()
    acc_ref[...] = jnp.zeros_like(acc_ref)
    for load in loads[18:34]:
        load.wait()
    mine = lax.broadcasted_iota(jnp.int32, (128, 128), 1) == (y * 2 + c) * 16 + x * 4 + z
    found = jnp.where(mine, cells_ref[...], 0.0)
    found = jnp.broadcast_to(jnp.sum(found, axis=1, keepdims=True), (128, 128))
    hits_ref[...] = found.T[0:8, :].astype(jnp.int32)
    hits = pltpu.make_async_copy(hits_ref, hit_ref, fact_sem)
    hits.start()
    own = []
    for slot in range(8):
        a, b, live = (slots_ref[0, 0, slot, field] for field in range(3))
        dx, dz = ((b >> 2) - x) & 3, ((b & 3) - z) & 3
        s1, s2 = jnp.where(c == 0, dx, dz), jnp.where(c == 0, dz, dx)
        k = ((a & 1) ^ c) * 4 + (((a >> 1) - y) & 3)
        own.append((k + 8 * (s2 * 4 + s1) + 256 * (16 + k), live, jnp.where(s2 == 2, 1, 0)))
    hits.wait()
    n = jnp.int32(0)
    for far in (False, True):
        for entry, live, there in own:
            list_ref[n] = entry
            n = n + live * (there if far else 1 - there)
        for place in range(8, 12) if far else (*range(8), *range(12, 16)):
            for k in range(8):
                list_ref[n] = k + 8 * place + 128 + 256 * (16 + k)
                n = n + hit_ref[0, place * 8 + k]
        if not far:
            near = n
    list_ref[SLOTS_OUT - 2] = near
    list_ref[SLOTS_OUT - 1] = n
    for load in loads[0:18]:
        load.wait()
    facts = pltpu.make_async_copy(fin_ref, facts_ref, fact_sem)
    facts.start()
    for place in range(16):
        split_into(xs_ref, place, slice(None), x_ref[place])

    def saved(t):
        slot = t & 1
        return pltpu.make_async_copy(pair_ref.at[slot], store_ref.at[jnp.minimum(t, KEPT - 1)], save_sems.at[slot])

    def visit(t, carry):
        k, place, turned, block = unpack(list_ref[t])
        slot = t & 1

        @pl.when((t >= 2) & (t - 2 < KEPT))
        def _():
            saved(t - 2).wait()

        pair = pair_ref.at[slot]
        sums = make_tile(
            fin_ref[place, 0:64, :], fin_ref[place, 64:65, :], fin_ref[block, 0:64, :], fin_ref[block, 64:65, :],
            turned, lc_ref, e_ref, pair,
        )

        @pl.when(t < KEPT)
        def _():
            saved(t).start()

        add_product(xs_ref, place, pair, acc_ref, k)
        spread = jnp.concatenate([sums[:, g * 128 : g * 128 + 128] for g in range(4)] + [jnp.zeros((4, 128), F32)], axis=0)
        acc_ref[k, BODY:ROWS, :] += spread
        return carry

    lax.fori_loop(0, n, visit, jnp.int32(0))
    for back in (2, 1):

        @pl.when((n >= back) & (n - back < KEPT))
        def _():
            saved(n - back).wait()

    keep_ref[...] = acc_ref[0:4]
    other_ref[...] = acc_ref[4:8]
    facts.wait()


DEPTH = 4


def products(
    first, last, local, list_ref, lc_ref, store_ref, facts_ref,
    fin_ref, fout_ref, xs_ref, e_ref, pair_ref, acc_ref, sems, fact_sems, fill,
):
    kept = jnp.clip(KEPT, first, last)

    def loaded(t):
        slot = (t - first) & (DEPTH - 1)
        return pltpu.make_async_copy(store_ref.at[jnp.minimum(t, KEPT - 1)], pair_ref.at[slot], sems.at[slot])

    for ahead in range(DEPTH):

        @pl.when(first + ahead < kept)
        def _():
            loaded(first + ahead).start()

    fill()

    def visit(t, carry):
        k, place, _, _ = unpack(list_ref[t])
        loaded(t).wait()
        add_product(xs_ref, local(place), pair_ref.at[(t - first) & (DEPTH - 1)], acc_ref, k)

        @pl.when(t + DEPTH < kept)
        def _():
            loaded(t + DEPTH).start()

        return carry

    lax.fori_loop(first, kept, visit, jnp.int32(0))

    def visit_again(t, carry):
        k, place, turned, block = unpack(list_ref[t])
        one = pltpu.make_async_copy(facts_ref.at[place], fin_ref, fact_sems.at[0])
        two = pltpu.make_async_copy(facts_ref.at[block], fout_ref, fact_sems.at[1])
        one.start()
        two.start()
        one.wait()
        two.wait()
        pair = pair_ref.at[0]
        make_tile(fin_ref[0:64, :], fin_ref[64:65, :], fout_ref[0:64, :], fout_ref[64:65, :], turned, lc_ref, e_ref, pair)
        add_product(xs_ref, local(place), pair, acc_ref, k)
        return carry

    lax.fori_loop(kept, last, visit_again, jnp.int32(0))


def fill_from(pieces, xs_ref):
    sums = jnp.zeros((8, 128), F32)
    for q, piece in enumerate(pieces):
        for j in range(2):
            for g in range(4):
                split_into(xs_ref, 2 * q + j, slice(g * 128, g * 128 + 128), piece[j, g * 64 : g * 64 + 64, :])
            sums = sums + piece[j, BODY:ROWS, :]
    return sums


def near_kernel(
    list_ref, lc_ref, p0, p1, p2, p3, p6, p7, store_ref, facts_ref, acc_ref,
    fin_ref, fout_ref, xs_ref, e_ref, pair_ref, sems, fact_sems,
):
    def fill():
        acc_ref[...] = jnp.zeros_like(acc_ref)
        sums = fill_from((p0, p1, p2, p3, p6, p7), xs_ref)
        for k in range(8):
            acc_ref[k, BODY:ROWS, :] = sums

    products(
        jnp.int32(0), list_ref[SLOTS_OUT - 2], lambda p: jnp.where(p >= 12, p - 4, p),
        list_ref, lc_ref, store_ref, facts_ref,
        fin_ref, fout_ref, xs_ref, e_ref, pair_ref, acc_ref, sems, fact_sems, fill,
    )


def far_kernel(
    list_ref, lc_ref, p4, p5, near_ref, store_ref, facts_ref, keep_ref, other_ref,
    fin_ref, fout_ref, xs_ref, e_ref, pair_ref, acc_ref, sems, fact_sems,
):
    def fill():
        acc_ref[...] = near_ref[...]
        sums = fill_from((p4, p5), xs_ref)
        for k in range(8):
            acc_ref[k, BODY:ROWS, :] += sums

    products(
        list_ref[SLOTS_OUT - 2], list_ref[SLOTS_OUT - 1], lambda p: p - 8,
        list_ref, lc_ref, store_ref, facts_ref,
        fin_ref, fout_ref, xs_ref, e_ref, pair_ref, acc_ref, sems, fact_sems, fill,
    )
    keep_ref[...] = acc_ref[0:4]
    other_ref[...] = acc_ref[4:8]


def group(g):
    return slice(g * 64, g * 64 + 64)


def lanes(g):
    return slice(g * 128, g * 128 + 128)


def sum_rows(first, second):
    both = jnp.concatenate([first, second], axis=0)
    column = jnp.broadcast_to(jnp.sum(both, axis=1, keepdims=True), (128, 128))
    return column.T[0:8, :]


def columns_of(row):
    turned = jnp.broadcast_to(row, (128, 128)).T
    return turned[0:64], turned[64:128]


def total_of(parts, rows):
    a, b, c, d, e = (part[0, rows, :] for part in parts)
    return (a + b) + (c + d) + e


def after_first(a, b, c, d, e, r_ref, err_ref, w_ref, diag_ref):
    parts = (a, b, c, d, e)
    errors = jnp.concatenate([err_ref[:, lanes(g)] for g in range(4)], axis=0)
    diag = errors + total_of(parts, slice(BODY, BODY + 4))
    diag_ref[0:4, :] = diag
    diag_ref[4:8, :] = jnp.zeros((4, 128), F32)
    rr, rw = jnp.zeros((64, 128), F32), jnp.zeros((64, 128), F32)
    for g in range(4):
        r = r_ref[:, lanes(g)]
        w = diag[g : g + 1, :] * r + total_of(parts, group(g))
        w_ref[group(g), :] = w
        rr, rw = rr + r * r, rw + r * w
    w_ref[BODY:ROWS, :] = sum_rows(rr, rw)


def after_second(a, b, c, d, e, r_ref, w_ref, diag_ref, next_ref, r1_ref, q_ref, past_ref):
    parts = (a, b, c, d, e)
    rr0, rw0 = columns_of(total_of(parts, slice(BODY, BODY + 1)))
    alpha = rr0 / rw0
    past_ref[0:64, :] = alpha
    past_ref[64:128, :] = rr0
    rr, rw = jnp.zeros((64, 128), F32), jnp.zeros((64, 128), F32)
    for g in range(4):
        w0 = w_ref[group(g), :]
        q = diag_ref[g : g + 1, :] * w0 + total_of(parts, group(g))
        r = r_ref[:, lanes(g)] - alpha * w0
        w = w0 - alpha * q
        q_ref[group(g), :] = q
        r1_ref[group(g), :] = r
        next_ref[group(g), :] = w
        rr, rw = rr + r * r, rw + r * w
    next_ref[BODY:ROWS, :] = sum_rows(rr, rw)


def after_third(
    a, b, c, d, e, r_ref, w0_ref, diag_ref, w1_ref, r1_ref, q_ref, past_ref,
    sums_ref, r2_ref, w2_ref, s1_ref, p1_ref, x_ref, now_ref,
):
    parts = (a, b, c, d, e)
    rr1, rw1 = columns_of(total_of(parts, slice(BODY, BODY + 1)))
    alpha0, rr0 = past_ref[0:64, :], past_ref[64:128, :]
    beta = rr1 / rr0
    alpha = rr1 / (rw1 - beta * rr1 / alpha0)
    now_ref[0:64, :] = alpha
    now_ref[64:128, :] = rr1
    rr, rw = jnp.zeros((64, 128), F32), jnp.zeros((64, 128), F32)
    for g in range(4):
        w1, r1, r0 = w1_ref[group(g), :], r1_ref[group(g), :], r_ref[:, lanes(g)]
        q1 = diag_ref[g : g + 1, :] * w1 + total_of(parts, group(g))
        s = w1 + beta * w0_ref[group(g), :]
        z = q1 + beta * q_ref[group(g), :]
        p = r1 + beta * r0
        r = r1 - alpha * s
        w = w1 - alpha * z
        s1_ref[group(g), :] = s
        p1_ref[group(g), :] = p
        x_ref[group(g), :] = alpha0 * r0 + alpha * p
        r2_ref[group(g), :] = r
        w2_ref[group(g), :] = w
        rr, rw = rr + r * r, rw + r * w
    sums_ref[...] = sum_rows(rr, rw)


def finish(sums_ref, r2_ref, w2_ref, s1_ref, p1_ref, x_ref, now_ref, inc_ref, res_ref):
    rr2, rw2 = columns_of(sums_ref[...])
    alpha1, rr1 = now_ref[0:64, :], now_ref[64:128, :]
    beta = rr2 / rr1
    alpha = rr2 / (rw2 - beta * rr2 / alpha1)
    for g in range(4):
        r = r2_ref[group(g), :]
        p = r + beta * p1_ref[group(g), :]
        s = w2_ref[group(g), :] + beta * s1_ref[group(g), :]
        inc_ref[:, lanes(g)] = x_ref[group(g), :] + alpha * p
        res_ref[:, lanes(g)] = r - alpha * s


def pack_kernel(slots_ref, factors_ref, component_ref, values_ref, out_ref, facts_ref, label_ref, sems):
    loads = [
        pltpu.make_async_copy(component_ref, label_ref, sems.at[0]),
        pltpu.make_async_copy(factors_ref, out_ref.at[pl.ds(0, 64), :], sems.at[1]),
        pltpu.make_async_copy(values_ref, out_ref.at[pl.ds(72, 64), :], sems.at[2]),
    ]
    for load in loads:
        load.start()
    lane = lax.broadcasted_iota(jnp.int32, (8, TILE), 1)
    row = lax.broadcasted_iota(jnp.int32, (8, TILE), 0)
    cells = jnp.zeros((8, TILE), jnp.int32)
    for slot in range(8):
        cell = slots_ref[0, 0, slot, 0] * 16 + slots_ref[0, 0, slot, 1]
        cells = cells + jnp.where(lane == cell, slots_ref[0, 0, slot, 2], 0)
    for load in loads:
        load.wait()
    below = jnp.where(row == 0, label_ref[...], jnp.where(row == 1, cells, 0)).astype(F32)
    out_ref[64:72, :] = below
    facts_ref[0:64, :] = out_ref[0:64, :]
    facts_ref[64:72, :] = below


VMEM = pl.BlockSpec(memory_space=pltpu.VMEM)
SMEM = pl.BlockSpec(memory_space=pltpu.SMEM)
ANY = pl.BlockSpec(memory_space=pl.ANY)


FIRST = pl.BlockSpec((1, ROWS, 128), lambda i: (0, 0, 0))


def small_call(body, shapes, args, parts=()):
    out = [jax.ShapeDtypeStruct(s, F32) for s in shapes]
    return pl.pallas_call(
        body,
        out_shape=out,
        grid=(1,),
        in_specs=[FIRST] * len(parts) + [VMEM] * len(args),
        out_specs=[VMEM] * len(shapes),
        compiler_params=pltpu.CompilerParams(vmem_limit_bytes=12 << 20),
        cost_estimate=pl.CostEstimate(flops=4_000_000, bytes_accessed=2_000_000, transcendentals=0),
    )(*parts, *args)


def pack(slots, factors, component, values):
    return pl.pallas_call(
        pack_kernel,
        out_shape=[jax.ShapeDtypeStruct((136, TILE), F32), jax.ShapeDtypeStruct((72, TILE), F32)],
        in_specs=[SMEM, ANY, ANY, ANY],
        out_specs=[VMEM, VMEM],
        scratch_shapes=[pltpu.VMEM((1, TILE), jnp.int32), pltpu.SemaphoreType.DMA((3,))],
        compiler_params=pltpu.CompilerParams(vmem_limit_bytes=4 << 20),
    )(slots, *[pltpu.with_memory_space_constraint(v, pltpu.HBM) for v in (factors, component, values)])


def laid(parts):
    height, total = parts[0].shape[0], 0.0
    for k, part in enumerate(parts):
        total = total + jnp.pad(part, ((k * height, (len(parts) - 1 - k) * height), (0, 0)))
    return total


PART = jax.ShapeDtypeStruct((4, ROWS, 128), F32)


ACC = jax.ShapeDtypeStruct((8, ROWS, 128), F32)


STORE = jax.ShapeDtypeStruct((KEPT, 2, TILE, TILE), BF16)


def first_operate(place, slots, log_coupling, pieces, cells, same, across):
    return pl.pallas_call(
        first_kernel,
        out_shape=[
            PART,
            PART,
            jax.ShapeDtypeStruct((SLOTS_OUT,), jnp.int32),
            STORE,
            jax.ShapeDtypeStruct((24, 72, TILE), F32),
        ],
        in_specs=[SMEM] * 3 + [ANY] * 11,
        out_specs=[VMEM, VMEM, SMEM, ANY, ANY],
        scratch_shapes=[
            pltpu.VMEM((24, 72, TILE), F32),
            pltpu.VMEM((16, 64, TILE), F32),
            pltpu.VMEM((16, 128, TILE), BF16),
            pltpu.VMEM((128, 128), F32),
            pltpu.VMEM((8, 128), jnp.int32),
            pltpu.SMEM((8, 128), jnp.int32),
            pltpu.VMEM((TILE, TILE), F32),
            pltpu.VMEM((2, 2, TILE, TILE), BF16),
            pltpu.VMEM((8, ROWS, 128), F32),
            pltpu.SemaphoreType.DMA,
            pltpu.SemaphoreType.DMA((42,)),
            pltpu.SemaphoreType.DMA((2,)),
        ],
        compiler_params=pltpu.CompilerParams(vmem_limit_bytes=18 << 20),
        cost_estimate=pl.CostEstimate(flops=8_000_000_000, bytes_accessed=20_000_000, transcendentals=2_000_000),
    )(place, slots, log_coupling, *pieces, cells, same, across)


def scratch(places):
    return [
        pltpu.VMEM((72, TILE), F32),
        pltpu.VMEM((72, TILE), F32),
        pltpu.VMEM((places, 128, TILE), BF16),
        pltpu.VMEM((TILE, TILE), F32),
        pltpu.VMEM((DEPTH, 2, TILE, TILE), BF16),
    ]


SEMS = [pltpu.SemaphoreType.DMA((DEPTH,)), pltpu.SemaphoreType.DMA((2,))]


def later_operate(listed, log_coupling, pieces, store, facts):
    near = pl.pallas_call(
        near_kernel,
        out_shape=ACC,
        in_specs=[SMEM, SMEM] + [VMEM] * 6 + [ANY] * 2,
        out_specs=VMEM,
        scratch_shapes=scratch(12) + SEMS,
        compiler_params=pltpu.CompilerParams(vmem_limit_bytes=14 << 20),
        cost_estimate=pl.CostEstimate(flops=3_000_000_000, bytes_accessed=12_000_000, transcendentals=0),
    )(listed, log_coupling, *pieces[0:4], *pieces[6:8], store, facts)
    return pl.pallas_call(
        far_kernel,
        out_shape=[PART, PART],
        in_specs=[SMEM, SMEM] + [VMEM] * 3 + [ANY] * 2,
        out_specs=[VMEM, VMEM],
        scratch_shapes=scratch(4) + [pltpu.VMEM((8, ROWS, 128), F32)] + SEMS,
        compiler_params=pltpu.CompilerParams(vmem_limit_bytes=14 << 20),
        cost_estimate=pl.CostEstimate(flops=1_000_000_000, bytes_accessed=6_000_000, transcendentals=0),
    )(listed, log_coupling, *pieces[4:6], near, store, facts)


def to_everyone(row, count, axes):
    copies = jnp.broadcast_to(row.reshape(1, 1, 128), (count, 1, 128))
    return lax.all_to_all(copies, axes, split_axis=0, concat_axis=0, tiled=True)


def shards(innovations, obs_factors, component, obs_error, coupling, tile_slots):
    place = jnp.stack([lax.axis_index(axis) for axis in ALL]).astype(jnp.int32)
    payload, facts = pack(tile_slots, obs_factors, component[None, :], innovations)
    same = jnp.stack([facts, shift_y(facts, -1), shift_y(facts, 2), shift_y(facts, 1)])
    across = swap_core(same)
    pieces = gather_row(payload)
    cells = laid([part[k, 65:66, 0:128] for part in (same, across) for k in range(4)])
    cells = jnp.broadcast_to(cells[None], (16, 8, 128))
    cells = lax.all_to_all(cells, ROW, split_axis=0, concat_axis=0, tiled=True)
    log_coupling = jnp.log2(coupling)
    error_row = obs_error[None, :]

    vec, body, two = (ROWS, 128), (BODY, 128), (128, 128)
    keep, other, listed, store, kept_facts = first_operate(place, tile_slots, log_coupling, pieces, cells, same, across)
    parts = reduce_col(keep, other)
    w0, diag = small_call(after_first, [vec, (8, 128)], (innovations, error_row), parts)

    keep, other = later_operate(listed, log_coupling, gather_row(w0), store, kept_facts)
    parts = reduce_col(keep, other)
    w1, r1, q0, past = small_call(after_second, [vec, body, body, two], (innovations, w0, diag), parts)

    keep, other = later_operate(listed, log_coupling, gather_row(w1), store, kept_facts)
    parts = reduce_col(keep, other)
    sums, r2, w2, s1, p1, x2, now = small_call(
        after_third,
        [(8, 128), body, body, body, body, body, two],
        (innovations, w0, diag, w1, r1, q0, past),
        parts,
    )
    sums = jnp.sum(to_everyone(sums[0:1], 128, ALL), axis=0)
    increment, residual = small_call(finish, [(64, TILE)] * 2, (sums, r2, w2, s1, p1, x2, now))
    return increment, residual


def solution(mesh):
    finer = Mesh(mesh.devices.reshape(4, 4, 4, 2), ALL)
    in_specs = (P(None, ALL), P(None, ALL), P(ALL), P(ALL), P(), P(ROW, COL, None, None))
    out_specs = (P(None, ALL), P(None, ALL))
    return jax.shard_map(shards, mesh=finer, in_specs=in_specs, out_specs=out_specs, check_vma=False)
```

```python
import functools
import math

import jax
import jax.numpy as jnp
from jax import lax
from jax.experimental import pallas as pl
from jax.experimental.pallas import tpu as pltpu
from jax.sharding import Mesh
from jax.sharding import PartitionSpec as P

TILE = 512
X, Z, Y, C = "row_0", "row_1", "col_0", "col_1"
ALL = (X, Z, Y, C)
ROW, COL = (X, Z), (Y, C)
BODY = 256
ROWS = BODY + 8
KEPT = 48
SLOTS_OUT = 144
KAPPA = math.log2(math.e) / 12.0
F32, BF16 = jnp.float32, jnp.bfloat16


def along_row(stage, step):
    pairs = []
    for x in range(4):
        for z in range(4):
            for y in range(4):
                for c in range(2):
                    if (c == 0) == (stage == 1):
                        to = ((x + step) % 4, z)
                    else:
                        to = (x, (z + step) % 4)
                    pairs.append((((x * 4 + z) * 4 + y) * 2 + c, ((to[0] * 4 + to[1]) * 4 + y) * 2 + c))
    return pairs


def hop(a, stage, step):
    return lax.ppermute(a, ALL, along_row(stage, step))


def gather_line(block):
    far = hop(block, 1, 2)
    ahead = hop(block, 1, -1)
    behind = hop(block, 1, 1)
    return block, ahead, far, behind


def gather_plane(line):
    low, high = jnp.stack(line[0:2]), jnp.stack(line[2:4])
    left_low = hop(low, 2, 1)
    right_high = hop(high, 2, -1)
    left_high = hop(high, 2, 1)
    right_low = hop(low, 2, -1)
    far_low = hop(left_low, 2, 1)
    far_high = hop(right_high, 2, -1)
    return low, high, right_low, right_high, far_low, far_high, left_low, left_high


def gather_row(block):
    return gather_plane(gather_line(block))


def swap_core(a):
    return lax.ppermute(a, C, [(0, 1), (1, 0)])


def shift_y(a, step):
    return lax.ppermute(a, Y, [(i, (i + step) % 4) for i in range(4)])


def reduce_col(keep, other):
    got = swap_core(other)
    one, two, three = [keep[j] + got[j] for j in (1, 2, 3)]
    far = shift_y(two, 2)
    return keep, got, shift_y(one, 1)[None], shift_y(three, -1)[None], far[None]


def halves(v):
    h = v.astype(BF16).astype(F32)
    m = (v - h).astype(BF16).astype(F32)
    return h, m, v - h - m


def rows_of(values, count, width):
    at = lax.broadcasted_iota(jnp.int32, (count, width), 0)
    out = jnp.zeros((count, width), F32)
    for k, value in enumerate(values):
        out = jnp.where(at == k, value, out)
    return out


def make_tile(fin, lin, fout, lout, turned, lc_ref, e_ref, pair_ref):
    h, m, l = halves(fin)
    norms = halves(-KAPPA * jnp.sum(fin * fin, axis=0, keepdims=True))
    aug = rows_of([*norms, 1.0, 1.0, 1.0, *[1.0 - lin, lin] * 3], 16, TILE)
    hm = jnp.concatenate([h, m], axis=0).T.astype(BF16)
    hl = jnp.concatenate([h, l], axis=0).T.astype(BF16)
    au = jnp.concatenate([aug, jnp.zeros((112, TILE), F32)], axis=0).T.astype(BF16)
    left = jnp.concatenate([hm, hm, hl, au], axis=1)
    g, n, k = halves(fout * (2.0 * KAPPA))
    norms = halves(-KAPPA * jnp.sum(fout * fout, axis=0, keepdims=True))
    levels = []
    for i in range(2):
        first = jnp.where(turned, lc_ref[i, 0], lc_ref[0, i])
        second = jnp.where(turned, lc_ref[i, 1], lc_ref[1, i])
        levels.append(halves(jnp.where(lout > 0.5, second, first)))
    logs = [levels[i][j] for j in range(3) for i in range(2)]
    aug = rows_of([1.0, 1.0, 1.0, *norms, *logs], 16, TILE)
    right = jnp.concatenate([g, g, n, n, k, g, aug, jnp.zeros((112, TILE), F32)], axis=0).astype(BF16)
    e_ref[...] = jnp.dot(left, right, preferred_element_type=F32)
    total = jnp.zeros((8, TILE), F32)
    for at in range(0, TILE, 64):
        t = jnp.exp2(e_ref[at : at + 64, :])
        hi = t.astype(BF16)
        pair_ref[0, at : at + 64, :] = hi
        pair_ref[1, at : at + 64, :] = (t - hi.astype(F32)).astype(BF16)
        total = total + jnp.sum(t.reshape(8, 8, TILE), axis=0)
    return jnp.sum(total, axis=0, keepdims=True)


def add_product(xs_ref, place, pair_ref, acc_ref, k):
    x = xs_ref[place]
    both = jnp.dot(x, pair_ref[0], preferred_element_type=F32)
    low = jnp.dot(x[:64], pair_ref[1], preferred_element_type=F32)
    out = both[:64] + both[64:] + low
    for g in range(4):
        acc_ref[k, g * 64 : g * 64 + 64, :] += out[:, g * 128 : g * 128 + 128]


def split_into(xs_ref, place, lanes, value):
    hi = value.astype(BF16)
    xs_ref[place, 0:64, lanes] = hi
    xs_ref[place, 64:128, lanes] = (value - hi.astype(F32)).astype(BF16)


def unpack(entry):
    return entry & 7, (entry >> 3) & 15, ((entry >> 7) & 1) == 1, entry >> 8


def first_kernel(
    place_ref, slots_ref, lc_ref, p0, p1, p2, p3, p4, p5, p6, p7, cells, same, across,
    keep_ref, other_ref, list_ref, store_ref, facts_ref,
    fin_ref, x_ref, xs_ref, cells_ref, hits_ref, hit_ref, e_ref, pair_ref, acc_ref, fact_sem, load_sems, save_sems,
):
    loads = []
    for q, piece in enumerate((p0, p1, p2, p3, p4, p5, p6, p7)):
        at = pl.ds(2 * q, 2)
        loads.append(pltpu.make_async_copy(piece.at[:, pl.ds(0, 72), :], fin_ref.at[at], load_sems.at[8 + q]))
        loads.append(pltpu.make_async_copy(piece.at[:, pl.ds(72, 64), :], x_ref.at[at], load_sems.at[16 + q]))
    loads.append(pltpu.make_async_copy(same, fin_ref.at[pl.ds(16, 4)], load_sems.at[24]))
    loads.append(pltpu.make_async_copy(across, fin_ref.at[pl.ds(20, 4)], load_sems.at[25]))
    x, z, y, c = (place_ref[axis] for axis in range(4))
    for place in range(16):
        s1, s2 = place & 3, place >> 2
        dx, dz = jnp.where(c == 0, s1, s2), jnp.where(c == 0, s2, s1)
        row = ((x + dx) & 3) * 4 + ((z + dz) & 3)
        loads.append(pltpu.make_async_copy(cells.at[row], cells_ref.at[pl.ds(8 * place, 8)], load_sems.at[26 + place]))
    for load in loads:
        load.start()
    acc_ref[...] = jnp.zeros_like(acc_ref)
    for load in loads[18:34]:
        load.wait()
    mine = lax.broadcasted_iota(jnp.int32, (128, 128), 1) == (y * 2 + c) * 16 + x * 4 + z
    found = jnp.where(mine, cells_ref[...], 0.0)
    found = jnp.broadcast_to(jnp.sum(found, axis=1, keepdims=True), (128, 128))
    hits_ref[...] = found.T[0:8, :].astype(jnp.int32)
    hits = pltpu.make_async_copy(hits_ref, hit_ref, fact_sem)
    hits.start()
    own = []
    for slot in range(8):
        a, b, live = (slots_ref[0, 0, slot, field] for field in range(3))
        dx, dz = ((b >> 2) - x) & 3, ((b & 3) - z) & 3
        s1, s2 = jnp.where(c == 0, dx, dz), jnp.where(c == 0, dz, dx)
        k = ((a & 1) ^ c) * 4 + (((a >> 1) - y) & 3)
        own.append((k + 8 * (s2 * 4 + s1) + 256 * (16 + k), live, jnp.where(s2 == 2, 1, 0)))
    hits.wait()
    n = jnp.int32(0)
    for far in (False, True):
        for entry, live, there in own:
            list_ref[n] = entry
            n = n + live * (there if far else 1 - there)
        for place in range(8, 12) if far else (*range(8), *range(12, 16)):
            for k in range(8):
                list_ref[n] = k + 8 * place + 128 + 256 * (16 + k)
                n = n + hit_ref[0, place * 8 + k]
        if not far:
            near = n
    list_ref[SLOTS_OUT - 2] = near
    list_ref[SLOTS_OUT - 1] = n
    for load in loads[0:18]:
        load.wait()

    @pl.when(n > KEPT)
    def _():
        facts = pltpu.make_async_copy(fin_ref, facts_ref, fact_sem)
        facts.start()
        facts.wait()

    for place in range(16):
        split_into(xs_ref, place, slice(None), x_ref[place])

    def saved(t):
        slot = t & 1
        return pltpu.make_async_copy(pair_ref.at[slot], store_ref.at[jnp.minimum(t, KEPT - 1)], save_sems.at[slot])

    def visit(t, carry):
        k, place, turned, block = unpack(list_ref[t])
        slot = t & 1

        @pl.when((t >= 2) & (t - 2 < KEPT))
        def _():
            saved(t - 2).wait()

        pair = pair_ref.at[slot]
        sums = make_tile(
            fin_ref[place, 0:64, :], fin_ref[place, 64:65, :], fin_ref[block, 0:64, :], fin_ref[block, 64:65, :],
            turned, lc_ref, e_ref, pair,
        )

        @pl.when(t < KEPT)
        def _():
            saved(t).start()

        add_product(xs_ref, place, pair, acc_ref, k)
        spread = jnp.concatenate([sums[:, g * 128 : g * 128 + 128] for g in range(4)] + [jnp.zeros((4, 128), F32)], axis=0)
        acc_ref[k, BODY:ROWS, :] += spread
        return carry

    lax.fori_loop(0, n, visit, jnp.int32(0))
    for back in (2, 1):

        @pl.when((n >= back) & (n - back < KEPT))
        def _():
            saved(n - back).wait()

    keep_ref[...] = acc_ref[0:4]
    other_ref[...] = acc_ref[4:8]


DEPTH = 4


def products(
    first, last, local, list_ref, lc_ref, store_ref, facts_ref,
    fin_ref, fout_ref, xs_ref, e_ref, pair_ref, acc_ref, sems, fact_sems, fill,
):
    kept = jnp.clip(KEPT, first, last)

    def loaded(t):
        slot = (t - first) & (DEPTH - 1)
        return pltpu.make_async_copy(store_ref.at[jnp.minimum(t, KEPT - 1)], pair_ref.at[slot], sems.at[slot])

    for ahead in range(DEPTH):

        @pl.when(first + ahead < kept)
        def _():
            loaded(first + ahead).start()

    fill()

    def visit(t, carry):
        k, place, _, _ = unpack(list_ref[t])
        loaded(t).wait()
        add_product(xs_ref, local(place), pair_ref.at[(t - first) & (DEPTH - 1)], acc_ref, k)

        @pl.when(t + DEPTH < kept)
        def _():
            loaded(t + DEPTH).start()

        return carry

    lax.fori_loop(first, kept, visit, jnp.int32(0))

    def visit_again(t, carry):
        k, place, turned, block = unpack(list_ref[t])
        one = pltpu.make_async_copy(facts_ref.at[place], fin_ref, fact_sems.at[0])
        two = pltpu.make_async_copy(facts_ref.at[block], fout_ref, fact_sems.at[1])
        one.start()
        two.start()
        one.wait()
        two.wait()
        pair = pair_ref.at[0]
        make_tile(fin_ref[0:64, :], fin_ref[64:65, :], fout_ref[0:64, :], fout_ref[64:65, :], turned, lc_ref, e_ref, pair)
        add_product(xs_ref, local(place), pair, acc_ref, k)
        return carry

    lax.fori_loop(kept, last, visit_again, jnp.int32(0))


def fill_from(pieces, xs_ref):
    sums = jnp.zeros((8, 128), F32)
    for q, piece in enumerate(pieces):
        for j in range(2):
            for g in range(4):
                split_into(xs_ref, 2 * q + j, slice(g * 128, g * 128 + 128), piece[j, g * 64 : g * 64 + 64, :])
            sums = sums + piece[j, BODY:ROWS, :]
    return sums


def near_kernel(
    list_ref, lc_ref, p0, p1, p2, p3, p6, p7, store_ref, facts_ref, acc_ref,
    fin_ref, fout_ref, xs_ref, e_ref, pair_ref, sems, fact_sems,
):
    def fill():
        acc_ref[...] = jnp.zeros_like(acc_ref)
        sums = fill_from((p0, p1, p2, p3, p6, p7), xs_ref)
        for k in range(8):
            acc_ref[k, BODY:ROWS, :] = sums

    products(
        jnp.int32(0), list_ref[SLOTS_OUT - 2], lambda p: jnp.where(p >= 12, p - 4, p),
        list_ref, lc_ref, store_ref, facts_ref,
        fin_ref, fout_ref, xs_ref, e_ref, pair_ref, acc_ref, sems, fact_sems, fill,
    )


def far_kernel(
    list_ref, lc_ref, p4, p5, near_ref, store_ref, facts_ref, keep_ref, other_ref,
    fin_ref, fout_ref, xs_ref, e_ref, pair_ref, acc_ref, sems, fact_sems,
):
    def fill():
        acc_ref[...] = near_ref[...]
        sums = fill_from((p4, p5), xs_ref)
        for k in range(8):
            acc_ref[k, BODY:ROWS, :] += sums

    products(
        list_ref[SLOTS_OUT - 2], list_ref[SLOTS_OUT - 1], lambda p: p - 8,
        list_ref, lc_ref, store_ref, facts_ref,
        fin_ref, fout_ref, xs_ref, e_ref, pair_ref, acc_ref, sems, fact_sems, fill,
    )
    keep_ref[...] = acc_ref[0:4]
    other_ref[...] = acc_ref[4:8]


def group(g):
    return slice(g * 64, g * 64 + 64)


def lanes(g):
    return slice(g * 128, g * 128 + 128)


def sum_rows(first, second):
    both = jnp.concatenate([first, second], axis=0)
    column = jnp.broadcast_to(jnp.sum(both, axis=1, keepdims=True), (128, 128))
    return column.T[0:8, :]


def columns_of(row):
    turned = jnp.broadcast_to(row, (128, 128)).T
    return turned[0:64], turned[64:128]


def total_of(parts, rows):
    a, b, c, d, e = (part[0, rows, :] for part in parts)
    return (a + b) + (c + d) + e


def after_first(a, b, c, d, e, r_ref, err_ref, w_ref, diag_ref):
    parts = (a, b, c, d, e)
    errors = jnp.concatenate([err_ref[:, lanes(g)] for g in range(4)], axis=0)
    diag = errors + total_of(parts, slice(BODY, BODY + 4))
    diag_ref[0:4, :] = diag
    diag_ref[4:8, :] = jnp.zeros((4, 128), F32)
    rr, rw = jnp.zeros((64, 128), F32), jnp.zeros((64, 128), F32)
    for g in range(4):
        r = r_ref[:, lanes(g)]
        w = diag[g : g + 1, :] * r + total_of(parts, group(g))
        w_ref[group(g), :] = w
        rr, rw = rr + r * r, rw + r * w
    w_ref[BODY:ROWS, :] = sum_rows(rr, rw)


def after_second(a, b, c, d, e, r_ref, w_ref, diag_ref, next_ref, r1_ref, q_ref, past_ref):
    parts = (a, b, c, d, e)
    rr0, rw0 = columns_of(total_of(parts, slice(BODY, BODY + 1)))
    alpha = rr0 / rw0
    past_ref[0:64, :] = alpha
    past_ref[64:128, :] = rr0
    rr, rw = jnp.zeros((64, 128), F32), jnp.zeros((64, 128), F32)
    for g in range(4):
        w0 = w_ref[group(g), :]
        q = diag_ref[g : g + 1, :] * w0 + total_of(parts, group(g))
        r = r_ref[:, lanes(g)] - alpha * w0
        w = w0 - alpha * q
        q_ref[group(g), :] = q
        r1_ref[group(g), :] = r
        next_ref[group(g), :] = w
        rr, rw = rr + r * r, rw + r * w
    next_ref[BODY:ROWS, :] = sum_rows(rr, rw)


def after_third(
    a, b, c, d, e, r_ref, w0_ref, diag_ref, w1_ref, r1_ref, q_ref, past_ref,
    sums_ref, r2_ref, w2_ref, s1_ref, p1_ref, x_ref, now_ref,
):
    parts = (a, b, c, d, e)
    rr1, rw1 = columns_of(total_of(parts, slice(BODY, BODY + 1)))
    alpha0, rr0 = past_ref[0:64, :], past_ref[64:128, :]
    beta = rr1 / rr0
    alpha = rr1 / (rw1 - beta * rr1 / alpha0)
    now_ref[0:64, :] = alpha
    now_ref[64:128, :] = rr1
    rr, rw = jnp.zeros((64, 128), F32), jnp.zeros((64, 128), F32)
    for g in range(4):
        w1, r1, r0 = w1_ref[group(g), :], r1_ref[group(g), :], r_ref[:, lanes(g)]
        q1 = diag_ref[g : g + 1, :] * w1 + total_of(parts, group(g))
        s = w1 + beta * w0_ref[group(g), :]
        z = q1 + beta * q_ref[group(g), :]
        p = r1 + beta * r0
        r = r1 - alpha * s
        w = w1 - alpha * z
        s1_ref[group(g), :] = s
        p1_ref[group(g), :] = p
        x_ref[group(g), :] = alpha0 * r0 + alpha * p
        r2_ref[group(g), :] = r
        w2_ref[group(g), :] = w
        rr, rw = rr + r * r, rw + r * w
    sums_ref[...] = sum_rows(rr, rw)


def finish(sums_ref, r2_ref, w2_ref, s1_ref, p1_ref, x_ref, now_ref, inc_ref, res_ref):
    rr2, rw2 = columns_of(sums_ref[...])
    alpha1, rr1 = now_ref[0:64, :], now_ref[64:128, :]
    beta = rr2 / rr1
    alpha = rr2 / (rw2 - beta * rr2 / alpha1)
    for g in range(4):
        r = r2_ref[group(g), :]
        p = r + beta * p1_ref[group(g), :]
        s = w2_ref[group(g), :] + beta * s1_ref[group(g), :]
        inc_ref[:, lanes(g)] = x_ref[group(g), :] + alpha * p
        res_ref[:, lanes(g)] = r - alpha * s


def pack_kernel(slots_ref, factors_ref, component_ref, values_ref, out_ref, facts_ref, label_ref, sems):
    loads = [
        pltpu.make_async_copy(component_ref, label_ref, sems.at[0]),
        pltpu.make_async_copy(factors_ref, out_ref.at[pl.ds(0, 64), :], sems.at[1]),
        pltpu.make_async_copy(values_ref, out_ref.at[pl.ds(72, 64), :], sems.at[2]),
    ]
    for load in loads:
        load.start()
    lane = lax.broadcasted_iota(jnp.int32, (8, TILE), 1)
    row = lax.broadcasted_iota(jnp.int32, (8, TILE), 0)
    cells = jnp.zeros((8, TILE), jnp.int32)
    for slot in range(8):
        cell = slots_ref[0, 0, slot, 0] * 16 + slots_ref[0, 0, slot, 1]
        cells = cells + jnp.where(lane == cell, slots_ref[0, 0, slot, 2], 0)
    for load in loads:
        load.wait()
    below = jnp.where(row == 0, label_ref[...], jnp.where(row == 1, cells, 0)).astype(F32)
    out_ref[64:72, :] = below
    facts_ref[0:64, :] = out_ref[0:64, :]
    facts_ref[64:72, :] = below


VMEM = pl.BlockSpec(memory_space=pltpu.VMEM)
SMEM = pl.BlockSpec(memory_space=pltpu.SMEM)
ANY = pl.BlockSpec(memory_space=pl.ANY)


FIRST = pl.BlockSpec((1, ROWS, 128), lambda i: (0, 0, 0))


def small_call(body, shapes, args, parts=()):
    out = [jax.ShapeDtypeStruct(s, F32) for s in shapes]
    return pl.pallas_call(
        body,
        out_shape=out,
        grid=(1,),
        in_specs=[FIRST] * len(parts) + [VMEM] * len(args),
        out_specs=[VMEM] * len(shapes),
        compiler_params=pltpu.CompilerParams(vmem_limit_bytes=12 << 20),
        cost_estimate=pl.CostEstimate(flops=4_000_000, bytes_accessed=2_000_000, transcendentals=0),
    )(*parts, *args)


def pack(slots, factors, component, values):
    return pl.pallas_call(
        pack_kernel,
        out_shape=[jax.ShapeDtypeStruct((136, TILE), F32), jax.ShapeDtypeStruct((72, TILE), F32)],
        in_specs=[SMEM, ANY, ANY, ANY],
        out_specs=[VMEM, VMEM],
        scratch_shapes=[pltpu.VMEM((1, TILE), jnp.int32), pltpu.SemaphoreType.DMA((3,))],
        compiler_params=pltpu.CompilerParams(vmem_limit_bytes=4 << 20),
    )(slots, *[pltpu.with_memory_space_constraint(v, pltpu.HBM) for v in (factors, component, values)])


def laid(parts):
    height, total = parts[0].shape[0], 0.0
    for k, part in enumerate(parts):
        total = total + jnp.pad(part, ((k * height, (len(parts) - 1 - k) * height), (0, 0)))
    return total


PART = jax.ShapeDtypeStruct((4, ROWS, 128), F32)


ACC = jax.ShapeDtypeStruct((8, ROWS, 128), F32)


STORE = jax.ShapeDtypeStruct((KEPT, 2, TILE, TILE), BF16)


def first_operate(place, slots, log_coupling, pieces, cells, same, across):
    return pl.pallas_call(
        first_kernel,
        out_shape=[
            PART,
            PART,
            jax.ShapeDtypeStruct((SLOTS_OUT,), jnp.int32),
            STORE,
            jax.ShapeDtypeStruct((24, 72, TILE), F32),
        ],
        in_specs=[SMEM] * 3 + [ANY] * 11,
        out_specs=[VMEM, VMEM, SMEM, ANY, ANY],
        scratch_shapes=[
            pltpu.VMEM((24, 72, TILE), F32),
            pltpu.VMEM((16, 64, TILE), F32),
            pltpu.VMEM((16, 128, TILE), BF16),
            pltpu.VMEM((128, 128), F32),
            pltpu.VMEM((8, 128), jnp.int32),
            pltpu.SMEM((8, 128), jnp.int32),
            pltpu.VMEM((TILE, TILE), F32),
            pltpu.VMEM((2, 2, TILE, TILE), BF16),
            pltpu.VMEM((8, ROWS, 128), F32),
            pltpu.SemaphoreType.DMA,
            pltpu.SemaphoreType.DMA((42,)),
            pltpu.SemaphoreType.DMA((2,)),
        ],
        compiler_params=pltpu.CompilerParams(vmem_limit_bytes=18 << 20),
        cost_estimate=pl.CostEstimate(flops=8_000_000_000, bytes_accessed=20_000_000, transcendentals=2_000_000),
    )(place, slots, log_coupling, *pieces, cells, same, across)


def scratch(places):
    return [
        pltpu.VMEM((72, TILE), F32),
        pltpu.VMEM((72, TILE), F32),
        pltpu.VMEM((places, 128, TILE), BF16),
        pltpu.VMEM((TILE, TILE), F32),
        pltpu.VMEM((DEPTH, 2, TILE, TILE), BF16),
    ]


SEMS = [pltpu.SemaphoreType.DMA((DEPTH,)), pltpu.SemaphoreType.DMA((2,))]


def later_operate(listed, log_coupling, pieces, store, facts):
    near = pl.pallas_call(
        near_kernel,
        out_shape=ACC,
        in_specs=[SMEM, SMEM] + [VMEM] * 6 + [ANY] * 2,
        out_specs=VMEM,
        scratch_shapes=scratch(12) + SEMS,
        compiler_params=pltpu.CompilerParams(vmem_limit_bytes=14 << 20),
        cost_estimate=pl.CostEstimate(flops=3_000_000_000, bytes_accessed=12_000_000, transcendentals=0),
    )(listed, log_coupling, *pieces[0:4], *pieces[6:8], store, facts)
    return pl.pallas_call(
        far_kernel,
        out_shape=[PART, PART],
        in_specs=[SMEM, SMEM] + [VMEM] * 3 + [ANY] * 2,
        out_specs=[VMEM, VMEM],
        scratch_shapes=scratch(4) + [pltpu.VMEM((8, ROWS, 128), F32)] + SEMS,
        compiler_params=pltpu.CompilerParams(vmem_limit_bytes=14 << 20),
        cost_estimate=pl.CostEstimate(flops=1_000_000_000, bytes_accessed=6_000_000, transcendentals=0),
    )(listed, log_coupling, *pieces[4:6], near, store, facts)


def to_everyone(row, count, axes):
    copies = jnp.broadcast_to(row.reshape(1, 1, 128), (count, 1, 128))
    return lax.all_to_all(copies, axes, split_axis=0, concat_axis=0, tiled=True)


def shards(innovations, obs_factors, component, obs_error, coupling, tile_slots):
    place = jnp.stack([lax.axis_index(axis) for axis in ALL]).astype(jnp.int32)
    payload, facts = pack(tile_slots, obs_factors, component[None, :], innovations)
    same = jnp.stack([facts, shift_y(facts, -1), shift_y(facts, 2), shift_y(facts, 1)])
    across = swap_core(same)
    pieces = gather_row(payload)
    cells = laid([part[k, 65:66, 0:128] for part in (same, across) for k in range(4)])
    cells = jnp.broadcast_to(cells[None], (16, 8, 128))
    cells = lax.all_to_all(cells, ROW, split_axis=0, concat_axis=0, tiled=True)
    log_coupling = jnp.log2(coupling)
    error_row = obs_error[None, :]

    vec, body, two = (ROWS, 128), (BODY, 128), (128, 128)
    keep, other, listed, store, kept_facts = first_operate(place, tile_slots, log_coupling, pieces, cells, same, across)
    parts = reduce_col(keep, other)
    w0, diag = small_call(after_first, [vec, (8, 128)], (innovations, error_row), parts)

    keep, other = later_operate(listed, log_coupling, gather_row(w0), store, kept_facts)
    parts = reduce_col(keep, other)
    w1, r1, q0, past = small_call(after_second, [vec, body, body, two], (innovations, w0, diag), parts)

    keep, other = later_operate(listed, log_coupling, gather_row(w1), store, kept_facts)
    parts = reduce_col(keep, other)
    sums, r2, w2, s1, p1, x2, now = small_call(
        after_third,
        [(8, 128), body, body, body, body, body, two],
        (innovations, w0, diag, w1, r1, q0, past),
        parts,
    )
    sums = jnp.sum(to_everyone(sums[0:1], 128, ALL), axis=0)
    increment, residual = small_call(finish, [(64, TILE)] * 2, (sums, r2, w2, s1, p1, x2, now))
    return increment, residual


def solution(mesh):
    finer = Mesh(mesh.devices.reshape(4, 4, 4, 2), ALL)
    in_specs = (P(None, ALL), P(None, ALL), P(ALL), P(ALL), P(), P(ROW, COL, None, None))
    out_specs = (P(None, ALL), P(None, ALL))
    return jax.shard_map(shards, mesh=finer, in_specs=in_specs, out_specs=out_specs, check_vma=False)
```
